32 devices in a mesh: gx: 4 (over y, core), gy: 8 (over z, x).
Axes of the slice: x: 2, y: 2, z: 4, core: 2. Of those that a mesh axis runs over, the one named last changes fastest.
Arguments:
- points: bfloat16 [32768, 64], P(('gx', 'gy')), may hold values from -25 to 25
- solution: float32 [32768, 32], P(('gx', 'gy')), may hold values from -6 to 6
- residual: float32 [32768, 32], P(('gx', 'gy')), may hold values from -36 to 36
- near_leaves: int32 [64, 4], P(('gx', 'gy')), may hold values from 0 to 63, as said below
- node_skeleton: int32 [32, 128], P(('gx', 'gy')), may hold values from 0 to 1023, as said below
- upper_skeleton: int32 [31, 128], replicated, may hold values from 0 to 255, as said below
- far_nodes: int32 [64, 16], P(('gx', 'gy')), may hold values from 0 to 62, as said below
Outputs:
- solution_next: float32 [32768, 32], P(('gx', 'gy'))
- residual_next: float32 [32768, 32], P(('gx', 'gy'))
- matvec_image: float32 [32768, 32], P(('gx', 'gy'))
The draws below stay inside these ranges and needn't reach their ends.
Inputs may be any that keep to these rules, and one draw needn't show every extreme that they name: `near_leaves`: leaves are numbered in point order, 2 to a device in the flat device order. A leaf's 4 near leaves are distinct and lie on other devices of its gx row; the near leaves named by one device's leaves are all distinct, at most 2 of them lie on any one other device, and exactly 2 on some. `node_skeleton`: each row holds 128 distinct positions among its device's 1024 points. `upper_skeleton`: row u holds 128 distinct positions among the 256 skeleton points of nodes 2u+1 and 2u+2, those of 2u+1 first. `far_nodes`: each row holds 16 distinct tree nodes.
All inputs are finite; a program needn't handle non-finite values.
Results may differ from the reference program's by a relative error of at most 0.0033.
Values may be sent and summed in bfloat16 or wider, within the bound.
No kernel may reach another device: no remote copies, remote signals or barrier semaphores. Data moves between devices by JAX's collectives and lax.ppermute only.
A program may use at most 128 MiB of HBM per device.

```python
import math
import jax
import jax.numpy as jnp
from jax import lax

D = 64
NRHS = 32
LEAF = 512
RANK = 128
NEAR = 4
FAR = 16
LEAF_DEV = 2
CPD = 1024
NPTS = 32768
LEAVES = 64
NODES = 63
N_GY = 8
DEVICES = 32


def draw_points(key, part):
    order = jax.random.permutation(jax.random.fold_in(key, 13), D).astype(jnp.float32)
    heavy = 36.0 * D / 64.0
    floor_var = 0.25
    base = jnp.clip(jax.random.normal(jax.random.fold_in(key, 17), (NPTS, D), jnp.float32), -4.0, 4.0)
    spread = jnp.sqrt(heavy * jnp.exp(-0.5 * order) + floor_var)
    return (base * spread[None, :]).astype(jnp.bfloat16)


def draw_residual(key, part):
    rise = 1.0 + 2.0 * jnp.arange(NPTS, dtype=jnp.float32)[:, None] / NPTS
    base = jnp.clip(jax.random.normal(key, (NPTS, NRHS), jnp.float32), -6.0, 6.0)
    return base * rise


def draw_near_leaves(key, part):
    request_total = LEAF_DEV * NEAR
    peer_count = N_GY - 1

    def one_device(device_key, device_number):
        shuffled = jax.random.permutation(jax.random.fold_in(device_key, 1), request_total)
        column = device_number % N_GY
        row_number = device_number // N_GY
        folded = shuffled % peer_count
        offset = 1 + (folded + N_GY // 2 - 1) % peer_count
        owner_slot = (column + offset) % N_GY
        request_order = jnp.arange(request_total)
        earlier = (owner_slot[:, None] == owner_slot[None, :]) & (request_order[None, :] < request_order[:, None])
        slot_number = jnp.sum(earlier.astype(jnp.int32), axis=1)
        starts = jax.random.randint(jax.random.fold_in(device_key, 2), (N_GY,), 0, LEAF_DEV)
        local_leaf = (starts[owner_slot] + slot_number) % LEAF_DEV
        return ((row_number * N_GY + owner_slot) * LEAF_DEV + local_leaf).astype(jnp.int32)
    device_keys = jax.random.split(jax.random.fold_in(key, 11), DEVICES)
    lists = jax.vmap(one_device)(device_keys, jnp.arange(DEVICES))
    return lists.reshape(LEAVES, NEAR)


def draw_node_skeleton(key, part):
    stride = CPD // RANK
    jitter = jax.random.randint(jax.random.fold_in(key, 3), (DEVICES, RANK), 0, stride)
    return (jnp.arange(RANK)[None, :] * stride + jitter).astype(jnp.int32)


def draw_upper_skeleton(key, part):
    choose_bits = jax.random.randint(jax.random.fold_in(key, 5), (DEVICES - 1, RANK), 0, 2)
    return (2 * jnp.arange(RANK)[None, :] + choose_bits).astype(jnp.int32)


def draw_far_nodes(key, part):
    spacing = NODES // FAR
    starts = jax.random.randint(jax.random.fold_in(key, 1), (LEAVES, 1), 0, NODES)
    jitter = jax.random.randint(jax.random.fold_in(key, 2), (LEAVES, FAR), 0, spacing)
    return ((starts + jnp.arange(FAR)[None, :] * spacing + jitter) % NODES).astype(jnp.int32)


def shard_levels(own_key, shape, cuts, low, top_value):
    gain = 1.0
    for axis_at, shards_of in cuts:
        steps = jax.random.uniform(jax.random.fold_in(jax.random.fold_in(own_key, 6), axis_at), (shards_of,), jnp.float32, low / len(cuts), top_value / len(cuts))
        gain = gain * jnp.repeat(jnp.exp(steps), shape[axis_at] // shards_of).reshape((-1,) + (1,) * (len(shape) - 1 - axis_at))
    return gain


def bell_draw(stream_key, extent, scale, most, cuts=(), kind=jnp.bfloat16):
    values = scale * jax.random.normal(stream_key, extent, jnp.float32)
    if cuts:
        values = values * shard_levels(stream_key, extent, cuts, -0.22, 0.18)
    return jnp.clip(values, -most, most).astype(kind)


def setup_inputs(seed: int = 0) -> dict:
    streams_of = jax.random.split(jax.random.key(seed), 8)
    return {
        "points": draw_points(jax.random.fold_in(streams_of[7], 71), 0),
        "solution": bell_draw(streams_of[1], (NPTS, NRHS), 1.0, 6.0, ((0, 32),), jnp.float32),
        "residual": draw_residual(jax.random.fold_in(streams_of[7], 71), 0),
        "near_leaves": draw_near_leaves(jax.random.fold_in(streams_of[7], 71), 0),
        "node_skeleton": draw_node_skeleton(jax.random.fold_in(streams_of[7], 71), 0),
        "upper_skeleton": draw_upper_skeleton(jax.random.fold_in(streams_of[7], 71), 0),
        "far_nodes": draw_far_nodes(jax.random.fold_in(streams_of[7], 71), 0),
    }


LAMBDA_RIDGE = 1.0
FULL_PRECISION = lax.Precision.HIGHEST

def kernel_tile(left_points, right_points):
    left_square = lax.optimization_barrier(jnp.sum(jnp.square(left_points.astype(jnp.float32)), axis=-1))
    right_square = lax.optimization_barrier(jnp.sum(jnp.square(right_points.astype(jnp.float32)), axis=-1))
    cross_term = jnp.dot(left_points, right_points.T, preferred_element_type=jnp.float32)
    distance = left_square[:, None] + right_square[None, :] - 2.0 * cross_term
    return jnp.exp(distance * (-0.5 / left_points.shape[-1]))

def kernel_batch(left_points, right_points):
    left_wide = left_points.astype(jnp.float32)
    right_wide = right_points.astype(jnp.float32)
    left_square = lax.optimization_barrier(jnp.sum(left_wide * left_wide, axis=-1))
    right_square = lax.optimization_barrier(jnp.sum(right_wide * right_wide, axis=-1))
    cross_term = jnp.einsum('bmd,bnd->bmn', left_wide, right_wide, precision=FULL_PRECISION)
    distance = left_square[:, :, None] + right_square[:, None, :] - 2.0 * cross_term
    return jnp.exp(distance * (-0.5 / left_points.shape[-1]))

def far_kernel(own_points, far_points):
    own_wide = own_points.astype(jnp.float32)
    far_wide = far_points.astype(jnp.float32)
    own_square = lax.optimization_barrier(jnp.sum(own_wide * own_wide, axis=-1))
    far_square = lax.optimization_barrier(jnp.sum(far_wide * far_wide, axis=-1))
    cross_term = jnp.einsum('id,frd->fir', own_wide, far_wide, precision=FULL_PRECISION)
    distance = own_square[None, :, None] + far_square[:, None, :] - 2.0 * cross_term
    return jnp.exp(distance * (-0.5 / own_points.shape[-1]))

def cholesky_solve(matrix, right_side):
    order = matrix.shape[0]
    indices = jnp.arange(order, dtype=jnp.int32)

    def unit(column):
        return (indices == column).astype(matrix.dtype)

    def factor_step(column, lower):
        pick = unit(column)
        matrix_column = jnp.dot(matrix, pick, precision=FULL_PRECISION)
        lower_row = jnp.dot(pick, lower, precision=FULL_PRECISION)
        remainder = matrix_column - jnp.dot(lower, lower_row, precision=FULL_PRECISION)
        pivot = jnp.sqrt(jnp.sum(remainder * pick))
        new_column = jnp.where(indices >= column, remainder / pivot, jnp.zeros_like(remainder))
        return lower + new_column[:, None] * pick[None, :]
    lower = lax.fori_loop(0, order, factor_step, jnp.zeros_like(matrix))
    diagonal_part = lax.optimization_barrier(jnp.sum(lower * jnp.eye(order, dtype=matrix.dtype), axis=1))

    def forward_step(column, partial_value):
        pick = unit(column)
        lower_row = jnp.dot(pick, lower, precision=FULL_PRECISION)
        value = (jnp.dot(pick, right_side, precision=FULL_PRECISION) - jnp.dot(lower_row, partial_value, precision=FULL_PRECISION)) / jnp.sum(diagonal_part * pick)
        return partial_value + pick[:, None] * value[None, :]
    half_solve = lax.fori_loop(0, order, forward_step, jnp.zeros_like(right_side))

    def backward_step(count, partial_value):
        column = order - 1 - count
        pick = unit(column)
        lower_column = jnp.dot(lower, pick, precision=FULL_PRECISION)
        value = (jnp.dot(pick, half_solve, precision=FULL_PRECISION) - jnp.dot(lower_column, partial_value, precision=FULL_PRECISION)) / jnp.sum(diagonal_part * pick)
        return partial_value + pick[:, None] * value[None, :]
    return lax.fori_loop(0, order, backward_step, jnp.zeros_like(right_side))

def build_levels(level_points, level_weights, upper_skeleton, level_top, level_stop, block_index):
    point_levels = [level_points]
    weight_levels = [level_weights]
    for level_now in range(level_top - 1, level_stop - 1, -1):
        half_count = level_points.shape[0] // 2
        child_points = level_points.reshape(half_count, 2 * level_points.shape[1], level_points.shape[2])
        child_weights = level_weights.reshape(half_count, 2 * level_weights.shape[1], level_weights.shape[2])
        pick_rows = lax.dynamic_slice_in_dim(upper_skeleton, 2 ** level_now - 1 + block_index * half_count, half_count, 0)
        level_points = jax.vmap(lambda group_points, group_picks: jnp.take(group_points, group_picks, axis=0))(child_points, pick_rows)
        transfer = kernel_batch(level_points, child_points)
        level_weights = jnp.einsum('bmn,bnc->bmc', transfer, child_weights, precision=FULL_PRECISION) / lax.optimization_barrier(jnp.sum(transfer, axis=2))[:, :, None]
        point_levels.insert(0, level_points)
        weight_levels.insert(0, level_weights)
    return (point_levels, weight_levels)

def leaf_image(own_points, near_points, near_values, far_points, far_weights):
    near_tiles = jax.vmap(lambda other_points: kernel_tile(own_points, other_points))(near_points).astype(jnp.bfloat16)
    near_part = jnp.einsum('nij,njc->ic', near_tiles.astype(jnp.float32), near_values.astype(jnp.float32), precision=FULL_PRECISION)
    far_tiles = far_kernel(own_points, far_points)
    far_part = jnp.einsum('fir,frc->ic', far_tiles, far_weights, precision=FULL_PRECISION)
    return near_part / math.sqrt(own_points.shape[0]) + far_part / far_points.shape[1]

def reference(points, solution, residual, near_leaves, node_skeleton, upper_skeleton, far_nodes):
    values_half = residual.astype(jnp.bfloat16)
    leaf_points = points.reshape(LEAVES, LEAF, D)
    leaf_values = values_half.reshape(LEAVES, LEAF, NRHS)

    def device_node(inputs):
        device_points, device_residual, skeleton_row = inputs
        skeleton_points = jnp.take(device_points, skeleton_row, axis=0)
        kernel = kernel_tile(skeleton_points, device_points)
        return (skeleton_points, jnp.dot(kernel, device_residual, precision=FULL_PRECISION) / math.sqrt(CPD))
    node_points, node_weights = lax.map(device_node, (points.reshape(DEVICES, CPD, D), residual.reshape(DEVICES, CPD, NRHS), node_skeleton))
    depth_total = DEVICES.bit_length() - 1
    point_levels, weight_levels = build_levels(node_points, node_weights, upper_skeleton, depth_total, 0, 0)
    tree_points = jnp.concatenate(point_levels, axis=0)
    tree_weights = jnp.concatenate(weight_levels, axis=0)

    def one_leaf(inputs):
        leaf_number, near_row, far_row = inputs
        own_points = leaf_points[leaf_number]
        near_points = jnp.concatenate([own_points[None], jnp.take(leaf_points, near_row, axis=0)], axis=0)
        near_values = jnp.concatenate([leaf_values[leaf_number][None], jnp.take(leaf_values, near_row, axis=0)], axis=0)
        return leaf_image(own_points, near_points, near_values, jnp.take(tree_points, far_row, axis=0), jnp.take(tree_weights, far_row, axis=0))
    leaf_terms = lax.map(one_leaf, (jnp.arange(LEAVES, dtype=jnp.int32), near_leaves, far_nodes))
    matvec_image = LAMBDA_RIDGE * residual + leaf_terms.reshape(NPTS, NRHS)
    gram_matrix = jnp.dot(matvec_image.T, matvec_image, precision=FULL_PRECISION)
    cross_product = jnp.dot(matvec_image.T, residual, precision=FULL_PRECISION)
    step_coeffs = cholesky_solve(gram_matrix, cross_product)
    solution_next = solution + jnp.dot(residual, step_coeffs, precision=FULL_PRECISION)
    residual_next = residual - jnp.dot(matvec_image, step_coeffs, precision=FULL_PRECISION)
    return (solution_next, residual_next, matvec_image)
```

```python
import functools
import math

import jax
import jax.numpy as jnp
from jax import lax
from jax.experimental import pallas as pl
from jax.experimental.pallas import tpu as pltpu
from jax.sharding import PartitionSpec as P

LAMBDA_RIDGE = 1.0
FULL = lax.Precision.HIGHEST
BF = jnp.bfloat16
F32 = jnp.float32
EXTRA = 16
NT = (((1,), (1,)), ((), ()))


def vmem(count):
    return [pl.BlockSpec(memory_space=pltpu.VMEM)] * count


def pieces(value):
    high = value.astype(BF).astype(F32)
    rest = value - high
    middle = rest.astype(BF).astype(F32)
    return high, middle, (rest - middle).astype(BF).astype(F32)


def square_rows(points):
    wide = points.astype(F32)
    return jnp.sum(wide * wide, axis=0, keepdims=True)


def left_block(points):
    count = points.shape[1]
    wide = points.astype(F32)
    square = jnp.sum(wide * wide, axis=0, keepdims=True)
    extra = jnp.concatenate(
        [*pieces(square), jnp.ones((3, count), F32), jnp.zeros((EXTRA - 6, count), F32)], axis=0
    )
    return jnp.concatenate([-2.0 * wide, extra], axis=0).T.astype(BF)


def right_extra(points):
    count = points.shape[1]
    return jnp.concatenate(
        [jnp.ones((3, count), F32), *pieces(square_rows(points)), jnp.zeros((EXTRA - 6, count), F32)],
        axis=0,
    ).astype(BF)


def kernel_of(left, right, depth):
    distance = jnp.dot(left, right, preferred_element_type=F32)
    return jnp.exp2(distance * (-0.5 * math.log2(math.e) / depth))


def skeleton_body(pick_ref, points_ref, residual_ref, block_ref, left_ref):
    depth, count = points_ref.shape
    rank = pick_ref.shape[1]
    points = points_ref[...]
    onehot = (lax.broadcasted_iota(jnp.int32, (count, rank), 0) == pick_ref[...]).astype(F32).astype(BF)
    chosen = jnp.dot(points, onehot, preferred_element_type=F32).astype(BF)
    right = jnp.concatenate([points, right_extra(points)], axis=0)
    tile = kernel_of(left_block(chosen), right, depth).astype(BF)
    weights = lax.dot_general(
        residual_ref[...].astype(BF), tile, NT, preferred_element_type=F32
    ) * (1.0 / math.sqrt(count))
    block = jnp.concatenate([chosen, weights.astype(BF)], axis=0)
    for copy in range(block_ref.shape[0]):
        block_ref[copy] = block
    left_ref[...] = left_block(points)


def tree_body(depth, upper_ref, *refs):
    part_refs, tree_ref = refs[:-1], refs[-1]
    row_total = len(part_refs)
    column_total = part_refs[0].shape[0]
    device_total = row_total * column_total
    first = device_total - 1
    rank = upper_ref.shape[1]
    mine = lax.axis_index("gx")

    def put(node, points, weights):
        tree_ref[node, :depth] = points
        tree_ref[node, depth : depth + EXTRA] = right_extra(points)
        tree_ref[node, depth + EXTRA :] = weights

    for slot, part_ref in enumerate(part_refs):
        row = lax.bitwise_xor(mine, slot)

        def place(column, carry, part_ref=part_ref, row=row):
            block = part_ref[column]
            put(first + row * column_total + column, block[:depth], block[depth:])
            return carry

        lax.fori_loop(0, column_total, place, 0, unroll=min(column_total, 8))

    ones = jnp.ones((EXTRA, 2 * rank), F32).astype(BF)
    low = (device_total - 1) // 2
    while True:
        count = low + 1

        def level(step, carry, low=low):
            node = low + step
            both = jnp.concatenate([tree_ref[2 * node + 1], tree_ref[2 * node + 2]], axis=1)
            points = both[:depth]
            values = jnp.concatenate([both[depth + EXTRA :], ones], axis=0)
            pick = upper_ref[pl.ds(node, 1), :]
            onehot = (lax.broadcasted_iota(jnp.int32, (2 * rank, rank), 0) == pick).astype(F32).astype(BF)
            chosen = jnp.dot(points, onehot, preferred_element_type=F32).astype(BF)
            tile = kernel_of(left_block(chosen), both[: depth + EXTRA], depth).astype(BF)
            sums = lax.dot_general(values, tile, NT, preferred_element_type=F32)
            width = values.shape[0] - EXTRA
            put(node, chosen, (sums[:width] / sums[width : width + 1]).astype(BF))
            return carry

        lax.fori_loop(0, count, level, 0, unroll=min(count, 4))
        if low == 0:
            break
        low = (low - 1) // 2


def far_body(leaf_dev, depth, far_ref, left_ref, tree_ref, own_ref, out_ref):
    leaf = left_ref.shape[0] // leaf_dev
    rank = tree_ref.shape[2]
    width = own_ref.shape[0] - depth
    far = far_ref.shape[1]
    for at in range(leaf_dev):
        left = left_ref[at * leaf : (at + 1) * leaf]
        own = own_ref[:, at * leaf : (at + 1) * leaf]
        right = jnp.concatenate([own[:depth], right_extra(own[:depth])], axis=0)
        tile = kernel_of(left, right, depth).astype(BF)
        near = lax.dot_general(tile, own[depth:], NT, preferred_element_type=F32)

        def step(pair, total, at=at, left=left):
            both = jnp.concatenate(
                [tree_ref[far_ref[at, 2 * pair]], tree_ref[far_ref[at, 2 * pair + 1]]], axis=1
            )
            tile = kernel_of(left, both[: depth + EXTRA], depth).astype(BF)
            return total + lax.dot_general(
                tile, both[depth + EXTRA :], NT, preferred_element_type=F32
            )

        total = lax.fori_loop(0, far // 2, step, jnp.zeros((leaf, width), F32), unroll=2)
        both = near * (1.0 / math.sqrt(leaf)) + total * (1.0 / rank)
        out_ref[:, at * leaf : (at + 1) * leaf] = both.T


def near_body(leaf_dev, depth, near_ref, left_ref, part_ref, residual_ref, *refs):
    block_refs = refs[:-5]
    image_ref, small_ref, held, sems, acc = refs[-5:]
    leaf = left_ref.shape[0] // leaf_dev
    near = near_ref.shape[1]
    mine = lax.axis_index("gy")
    columns = len(block_refs) + 1
    total = leaf_dev * near
    for request in range(total):
        wanted = near_ref[request // near, request % near]
        slot = lax.bitwise_xor(lax.rem(wanted // leaf_dev, columns), mine)
        inner = lax.rem(wanted, leaf_dev)
        for at, block_ref in enumerate(block_refs):

            @pl.when(slot == at + 1)
            def _(block_ref=block_ref, inner=inner, request=request):
                source = block_ref.at[:, pl.ds(pl.multiple_of(inner * leaf, leaf), leaf)]
                pltpu.make_async_copy(source, held.at[request], sems.at[request]).start()

    for at in range(leaf_dev):
        acc[...] = jnp.zeros_like(acc)

        def step(place, carry, at=at):
            request = at * near + place
            pltpu.make_async_copy(
                block_refs[0].at[:, :leaf], held.at[request], sems.at[request]
            ).wait()
            block = held[request]
            right = jnp.concatenate([block[:depth], right_extra(block[:depth])], axis=0)
            tile = kernel_of(left_ref[at * leaf : (at + 1) * leaf], right, depth).astype(BF)
            acc[...] += lax.dot_general(tile, block[depth:], NT, preferred_element_type=F32)
            return carry

        lax.fori_loop(0, near, step, 0)
        where = slice(at * leaf, (at + 1) * leaf)
        image_ref[:, where] = (
            LAMBDA_RIDGE * residual_ref[:, where]
            + part_ref[:, where]
            + acc[...].T * (1.0 / math.sqrt(leaf))
        )
    image = image_ref[...]
    gram = lax.dot_general(image, image, NT, precision=FULL, preferred_element_type=F32)
    cross = lax.dot_general(image, residual_ref[...], NT, precision=FULL, preferred_element_type=F32)
    half = gram.shape[0] // 2
    packed = jnp.concatenate([gram[:half], gram[half:], cross[:half], cross[half:]], axis=1)

    def copy(at, carry):
        small_ref[at] = packed
        return carry

    lax.fori_loop(0, small_ref.shape[0], copy, 0, unroll=8)


def solve_body(small_ref, solution_ref, residual_ref, image_ref, solution_out, residual_out):
    order = solution_ref.shape[0]
    half = order // 2
    packed = small_ref[0]
    for at in range(1, small_ref.shape[0]):
        packed = packed + small_ref[at]
    gram = jnp.concatenate([packed[:, :order], packed[:, order : 2 * order]], axis=0)
    cross = jnp.concatenate([packed[:, 2 * order : 3 * order], packed[:, 3 * order :]], axis=0)
    work = jnp.concatenate([gram, cross], axis=1)
    rows = lax.broadcasted_iota(jnp.int32, (order, 1), 0)
    for column in range(order):
        row = work[column : column + 1]
        inverse = 1.0 / jnp.sqrt(row[:, column : column + 1])
        factor = jnp.where(rows == column, 0.0, work[:, column : column + 1] * inverse)
        work = work - factor * (row * inverse)
    eye = (rows == lax.broadcasted_iota(jnp.int32, (order, order), 1)).astype(F32)
    diagonal = jnp.sum(work[:, :order] * eye, axis=1, keepdims=True)
    coeffs = (work[:, order:] / diagonal).T
    solution_out[...] = solution_ref[...] + jnp.dot(coeffs, residual_ref[...], precision=FULL, preferred_element_type=F32)
    residual_out[...] = residual_ref[...] - jnp.dot(coeffs, image_ref[...], precision=FULL, preferred_element_type=F32)


def cost(flops, exps, moved):
    return pl.CostEstimate(flops=int(flops), transcendentals=int(exps), bytes_accessed=int(moved))


def shards(points, solution, residual, near_leaves, node_skeleton, upper_skeleton, far_nodes):
    row_total = lax.axis_size("gx")
    column_total = lax.axis_size("gy")
    device_total = row_total * column_total
    leaf_dev = near_leaves.shape[0]
    near = near_leaves.shape[1]
    count, depth = points.shape
    width = residual.shape[1]
    leaf = count // leaf_dev
    rank = node_skeleton.shape[1]
    points_t = points.T
    residual_t = residual.T
    solution_t = solution.T
    near_block = jnp.concatenate([points_t, residual_t.astype(BF)], axis=0)
    near_blocks = [
        lax.ppermute(near_block, "gy", [(i, i ^ step) for i in range(column_total)])
        for step in range(1, column_total)
    ]
    deep = depth + EXTRA

    blocks, left = pl.pallas_call(
        skeleton_body,
        out_shape=(
            jax.ShapeDtypeStruct((column_total, depth + width, rank), BF),
            jax.ShapeDtypeStruct((count, deep), BF),
        ),
        in_specs=vmem(3),
        out_specs=tuple(vmem(2)),
        name="skeleton",
    )(node_skeleton, points_t, residual_t)
    mine = lax.all_to_all(blocks, "gy", 0, 0)
    parts = [mine]
    step = row_total // 2
    while step:
        swap = [(i, i ^ step) for i in range(row_total)]
        stacked = jnp.stack(parts) if len(parts) > 1 else parts[0][None]
        got = lax.ppermute(stacked, "gx", swap)
        parts = parts + [got[i] for i in range(len(parts))]
        step //= 2
    order = [0]
    step = row_total // 2
    while step:
        order = order + [o ^ step for o in order]
        step //= 2
    parts = [part for _, part in sorted(zip(order, parts), key=lambda pair: pair[0])]
    tree = pl.pallas_call(
        functools.partial(tree_body, depth),
        out_shape=jax.ShapeDtypeStruct((2 * device_total - 1, deep + width, rank), BF),
        in_specs=vmem(1 + row_total),
        out_specs=vmem(1)[0],
        name="tree",
    )(upper_skeleton, *parts)
    partial_t = pl.pallas_call(
        functools.partial(far_body, leaf_dev, depth),
        out_shape=jax.ShapeDtypeStruct((width, count), F32),
        in_specs=[pl.BlockSpec(memory_space=pltpu.SMEM), *vmem(3)],
        out_specs=vmem(1)[0],
        name="far",
    )(far_nodes, left, tree, near_block)
    image_t, small = pl.pallas_call(
        functools.partial(near_body, leaf_dev, depth),
        out_shape=(
            jax.ShapeDtypeStruct((width, count), F32),
            jax.ShapeDtypeStruct((device_total, width // 2, 4 * width), F32),
        ),
        in_specs=[
            pl.BlockSpec(memory_space=pltpu.SMEM),
            *vmem(3),
            *[pl.BlockSpec(memory_space=pl.ANY)] * (column_total - 1),
        ],
        out_specs=tuple(vmem(2)),
        scratch_shapes=[
            pltpu.VMEM((leaf_dev * near, depth + width, leaf), BF),
            pltpu.SemaphoreType.DMA((leaf_dev * near,)),
            pltpu.VMEM((leaf, width), F32),
        ],
        name="near",
    )(near_leaves, left, partial_t, residual_t, *near_blocks)
    small = lax.all_to_all(small, ("gx", "gy"), 0, 0)
    solution_next, residual_next = pl.pallas_call(
        solve_body,
        out_shape=(jax.ShapeDtypeStruct((width, count), F32),) * 2,
        in_specs=vmem(4),
        out_specs=tuple(vmem(2)),
        name="solve",
    )(small, solution_t, residual_t, image_t)
    return (solution_next.T, residual_next.T, image_t.T)


def solution(mesh):
    split = P(("gx", "gy"), None)
    return jax.shard_map(
        shards,
        mesh=mesh,
        in_specs=(split, split, split, split, split, P(), split),
        out_specs=(split, split, split),
        check_vma=False,
    )
```

```python
import functools
import math

import jax
import jax.numpy as jnp
from jax import lax
from jax.experimental import pallas as pl
from jax.experimental.pallas import tpu as pltpu
from jax.sharding import PartitionSpec as P


LAMBDA_RIDGE = 1.0
FULL = lax.Precision.HIGHEST
BF = jnp.bfloat16
F32 = jnp.float32
EXTRA = 16
GROUP = 16
NT = (((1,), (1,)), ((), ()))


def vmem(count):
    return [pl.BlockSpec(memory_space=pltpu.VMEM)] * count


def pieces(value):
    high = value.astype(BF).astype(F32)
    rest = value - high
    middle = rest.astype(BF).astype(F32)
    return high, middle, (rest - middle).astype(BF).astype(F32)


def square_rows(points):
    wide = points.astype(F32)
    return jnp.sum(wide * wide, axis=0, keepdims=True)


def left_block(points):
    count = points.shape[1]
    wide = points.astype(F32)
    square = jnp.sum(wide * wide, axis=0, keepdims=True)
    extra = jnp.concatenate(
        [*pieces(square), jnp.ones((3, count), F32), jnp.zeros((EXTRA - 6, count), F32)], axis=0
    )
    return jnp.concatenate([-2.0 * wide, extra], axis=0).T.astype(BF)


def right_extra(points):
    count = points.shape[1]
    return jnp.concatenate(
        [jnp.ones((3, count), F32), *pieces(square_rows(points)), jnp.zeros((EXTRA - 6, count), F32)],
        axis=0,
    ).astype(BF)


def kernel_of(left, right, depth):
    distance = jnp.dot(left, right, preferred_element_type=F32)
    return jnp.exp2(distance * (-0.5 * math.log2(math.e) / depth))


def skeleton_body(pick_ref, points_ref, residual_ref, block_ref, left_ref):
    depth, count = points_ref.shape
    rank = pick_ref.shape[1]
    points = points_ref[...]
    onehot = (lax.broadcasted_iota(jnp.int32, (count, rank), 0) == pick_ref[...]).astype(F32).astype(BF)
    chosen = jnp.dot(points, onehot, preferred_element_type=F32).astype(BF)
    right = jnp.concatenate([points, right_extra(points)], axis=0)
    tile = kernel_of(left_block(chosen), right, depth).astype(BF)
    weights = lax.dot_general(
        residual_ref[...].astype(BF), tile, NT, preferred_element_type=F32
    ) * (1.0 / math.sqrt(count))
    block = jnp.concatenate([chosen, weights.astype(BF)], axis=0)
    for copy in range(block_ref.shape[0]):
        block_ref[copy] = block
    left_ref[...] = left_block(points)


def tree_nodes(depth, upper_ref, tree_ref, nodes):
    rank = upper_ref.shape[1]
    lanes = lax.broadcasted_iota(jnp.int32, (2 * rank, rank), 0)
    both = [jnp.concatenate([tree_ref[2 * n + 1], tree_ref[2 * n + 2]], axis=1) for n in nodes]
    picks = [(lanes == upper_ref[pl.ds(n, 1), :]).astype(F32).astype(BF) for n in nodes]
    chosen = [
        jnp.dot(b[:depth], pick, preferred_element_type=F32).astype(BF) for b, pick in zip(both, picks)
    ]
    left = [left_block(points) for points in chosen]
    tiles = [kernel_of(l, b[: depth + EXTRA], depth).astype(BF) for l, b in zip(left, both)]
    ones = jnp.ones((EXTRA, 2 * rank), F32).astype(BF)
    values = [jnp.concatenate([b[depth + EXTRA :], ones], axis=0) for b in both]
    sums = [
        lax.dot_general(v, tile, NT, preferred_element_type=F32) for v, tile in zip(values, tiles)
    ]
    width = values[0].shape[0] - EXTRA
    weights = [(s[:width] / s[width : width + 1]).astype(BF) for s in sums]
    blocks = [
        jnp.concatenate([points, right_extra(points), w], axis=0)
        for points, w in zip(chosen, weights)
    ]
    for node, block in zip(nodes, blocks):
        tree_ref[node] = block


def tree_body(leaf_dev, depth, far_ref, upper_ref, left_ref, own_ref, *refs):
    part_refs, out_ref, tree_ref, acc = refs[:-3], refs[-3], refs[-2], refs[-1]
    row_total = len(part_refs)
    column_total = part_refs[0].shape[0]
    low = row_total * column_total - 1
    mine = lax.axis_index("gx")
    for slot, part_ref in enumerate(part_refs):
        first = low + lax.bitwise_xor(mine, slot) * column_total
        blocks = [part_ref[column] for column in range(column_total)]
        extras = [right_extra(block[:depth]) for block in blocks]
        for column, (block, extra) in enumerate(zip(blocks, extras)):
            tree_ref[first + column, :depth] = block[:depth]
            tree_ref[first + column, depth : depth + EXTRA] = extra
            tree_ref[first + column, depth + EXTRA :] = block[depth:]
    while low:
        low = (low - 1) // 2
        count = low + 1
        size = min(count, GROUP)

        def level(step, carry, low=low, size=size):
            tree_nodes(depth, upper_ref, tree_ref, [low + step * size + k for k in range(size)])
            return carry

        if count == size:
            level(0, 0)
        else:
            lax.fori_loop(0, count // size, level, 0)

    leaf = left_ref.shape[0] // leaf_dev
    rank = tree_ref.shape[2]
    far = far_ref.shape[1]
    for at in range(leaf_dev):
        where = slice(at * leaf, (at + 1) * leaf)
        own = own_ref[:, where]
        right = jnp.concatenate([own[:depth], right_extra(own[:depth])], axis=0)
        tile = kernel_of(left_ref[where], right, depth).astype(BF)
        acc[...] = lax.dot_general(tile, own[depth:], NT, preferred_element_type=F32) * (
            rank / math.sqrt(leaf)
        )

        def step(group, carry, at=at, where=where):
            nodes = [tree_ref[far_ref[at, 4 * group + k]] for k in range(4)]
            both = jnp.concatenate(nodes, axis=1)
            tile = kernel_of(left_ref[where], both[: depth + EXTRA], depth).astype(BF)
            acc[...] += lax.dot_general(tile, both[depth + EXTRA :], NT, preferred_element_type=F32)
            return carry

        lax.fori_loop(0, far // 4, step, 0)
        out_ref[:, where] = acc[...].T * (1.0 / rank)


def near_body(leaf_dev, depth, near_ref, left_ref, part_ref, residual_ref, *refs):
    block_refs = refs[:-5]
    image_ref, small_ref, held, sems, acc = refs[-5:]
    leaf = left_ref.shape[0] // leaf_dev
    near = near_ref.shape[1]
    mine = lax.axis_index("gy")
    columns = len(block_refs) + 1
    total = leaf_dev * near
    for request in range(total):
        wanted = near_ref[request // near, request % near]
        slot = lax.bitwise_xor(lax.rem(wanted // leaf_dev, columns), mine)
        inner = lax.rem(wanted, leaf_dev)
        for at, block_ref in enumerate(block_refs):

            @pl.when(slot == at + 1)
            def _(block_ref=block_ref, inner=inner, request=request):
                source = block_ref.at[:, pl.ds(pl.multiple_of(inner * leaf, leaf), leaf)]
                pltpu.make_async_copy(source, held.at[request], sems.at[request]).start()

    for at in range(leaf_dev):
        acc[...] = jnp.zeros_like(acc)

        def step(place, carry, at=at):
            request = at * near + place
            pltpu.make_async_copy(
                block_refs[0].at[:, :leaf], held.at[request], sems.at[request]
            ).wait()
            block = held[request]
            right = jnp.concatenate([block[:depth], right_extra(block[:depth])], axis=0)
            tile = kernel_of(left_ref[at * leaf : (at + 1) * leaf], right, depth).astype(BF)
            acc[...] += lax.dot_general(tile, block[depth:], NT, preferred_element_type=F32)
            return carry

        lax.fori_loop(0, near, step, 0)
        where = slice(at * leaf, (at + 1) * leaf)
        image_ref[:, where] = (
            LAMBDA_RIDGE * residual_ref[:, where]
            + part_ref[:, where]
            + acc[...].T * (1.0 / math.sqrt(leaf))
        )
    image = image_ref[...]
    gram = lax.dot_general(image, image, NT, precision=FULL, preferred_element_type=F32)
    cross = lax.dot_general(image, residual_ref[...], NT, precision=FULL, preferred_element_type=F32)
    half = gram.shape[0] // 2
    packed = jnp.concatenate([gram[:half], gram[half:], cross[:half], cross[half:]], axis=1)

    def copy(at, carry):
        small_ref[at] = packed
        return carry

    lax.fori_loop(0, small_ref.shape[0], copy, 0, unroll=8)


def solve_body(small_ref, solution_ref, residual_ref, image_ref, solution_out, residual_out):
    order = solution_ref.shape[0]
    packed = small_ref[0]
    for at in range(1, small_ref.shape[0]):
        packed = packed + small_ref[at]
    gram = jnp.concatenate([packed[:, :order], packed[:, order : 2 * order]], axis=0)
    cross = jnp.concatenate([packed[:, 2 * order : 3 * order], packed[:, 3 * order :]], axis=0)
    work = jnp.concatenate([gram, cross], axis=1)
    rows = lax.broadcasted_iota(jnp.int32, (order, 1), 0)
    for column in range(order):
        row = work[column : column + 1]
        inverse = 1.0 / jnp.sqrt(row[:, column : column + 1])
        factor = jnp.where(rows == column, 0.0, work[:, column : column + 1] * inverse)
        work = work - factor * (row * inverse)
    eye = (rows == lax.broadcasted_iota(jnp.int32, (order, order), 1)).astype(F32)
    diagonal = jnp.sum(work[:, :order] * eye, axis=1, keepdims=True)
    coeffs = (work[:, order:] / diagonal).T
    solution_out[...] = solution_ref[...] + jnp.dot(coeffs, residual_ref[...], precision=FULL, preferred_element_type=F32)
    residual_out[...] = residual_ref[...] - jnp.dot(coeffs, image_ref[...], precision=FULL, preferred_element_type=F32)


def step_of(points, solution, residual, near_leaves, node_skeleton, upper_skeleton, far_nodes):
    row_total = lax.axis_size("gx")
    column_total = lax.axis_size("gy")
    device_total = row_total * column_total
    leaf_dev = near_leaves.shape[0]
    near = near_leaves.shape[1]
    count, depth = points.shape
    width = residual.shape[1]
    leaf = count // leaf_dev
    rank = node_skeleton.shape[1]
    points_t = points.T
    residual_t = residual.T
    solution_t = solution.T
    near_block = jnp.concatenate([points_t, residual_t.astype(BF)], axis=0)
    near_blocks = [
        lax.ppermute(near_block, "gy", [(i, i ^ step) for i in range(column_total)])
        for step in range(1, column_total)
    ]
    deep = depth + EXTRA

    blocks, left = pl.pallas_call(
        skeleton_body,
        out_shape=(
            jax.ShapeDtypeStruct((column_total, depth + width, rank), BF),
            jax.ShapeDtypeStruct((count, deep), BF),
        ),
        in_specs=vmem(3),
        out_specs=tuple(vmem(2)),
        name="skeleton",
    )(node_skeleton, points_t, residual_t)
    mine = lax.all_to_all(blocks, "gy", 0, 0)
    parts = [mine]
    step = row_total // 2
    while step:
        swap = [(i, i ^ step) for i in range(row_total)]
        stacked = jnp.stack(parts) if len(parts) > 1 else parts[0][None]
        got = lax.ppermute(stacked, "gx", swap)
        parts = parts + [got[i] for i in range(len(parts))]
        step //= 2
    order = [0]
    step = row_total // 2
    while step:
        order = order + [o ^ step for o in order]
        step //= 2
    parts = [part for _, part in sorted(zip(order, parts), key=lambda pair: pair[0])]
    partial_t = pl.pallas_call(
        functools.partial(tree_body, leaf_dev, depth),
        out_shape=jax.ShapeDtypeStruct((width, count), F32),
        in_specs=[pl.BlockSpec(memory_space=pltpu.SMEM), *vmem(3 + row_total)],
        out_specs=vmem(1)[0],
        scratch_shapes=[
            pltpu.VMEM((2 * device_total - 1, deep + width, rank), BF),
            pltpu.VMEM((leaf, width), F32),
        ],
        name="tree",
    )(far_nodes, upper_skeleton, left, near_block, *parts)
    image_t, small = pl.pallas_call(
        functools.partial(near_body, leaf_dev, depth),
        out_shape=(
            jax.ShapeDtypeStruct((width, count), F32),
            jax.ShapeDtypeStruct((device_total, width // 2, 4 * width), F32),
        ),
        in_specs=[
            pl.BlockSpec(memory_space=pltpu.SMEM),
            *vmem(3 + column_total - 1),
        ],
        out_specs=tuple(vmem(2)),
        scratch_shapes=[
            pltpu.VMEM((leaf_dev * near, depth + width, leaf), BF),
            pltpu.SemaphoreType.DMA((leaf_dev * near,)),
            pltpu.VMEM((leaf, width), F32),
        ],
        name="near",
    )(near_leaves, left, partial_t, residual_t, *near_blocks)
    small = lax.all_to_all(small, ("gx", "gy"), 0, 0)
    solution_next, residual_next = pl.pallas_call(
        solve_body,
        out_shape=(jax.ShapeDtypeStruct((width, count), F32),) * 2,
        in_specs=vmem(4),
        out_specs=tuple(vmem(2)),
        name="solve",
    )(small, solution_t, residual_t, image_t)
    return (solution_next.T, residual_next.T, image_t.T)


def solution(mesh):
    split = P(("gx", "gy"), None)
    return jax.shard_map(
        step_of,
        mesh=mesh,
        in_specs=(split, split, split, split, split, P(), split),
        out_specs=(split, split, split),
        check_vma=False,
    )
```

```python
import functools
import math

import jax
import jax.numpy as jnp
from jax import lax
from jax.experimental import pallas as pl
from jax.experimental.pallas import tpu as pltpu
from jax.sharding import PartitionSpec as P


LAMBDA_RIDGE = 1.0
FULL = lax.Precision.HIGHEST
BF = jnp.bfloat16
F32 = jnp.float32
EXTRA = 16
GROUP = 16
GRANT = 24 * 2**20
NT = (((1,), (1,)), ((), ()))


def vmem(count):
    return [pl.BlockSpec(memory_space=pltpu.VMEM)] * count


def pieces(value):
    high = value.astype(BF).astype(F32)
    rest = value - high
    middle = rest.astype(BF).astype(F32)
    return high, middle, (rest - middle).astype(BF).astype(F32)


def square_rows(points):
    wide = points.astype(F32)
    return jnp.sum(wide * wide, axis=0, keepdims=True)


def left_block(points):
    count = points.shape[1]
    wide = points.astype(F32)
    square = jnp.sum(wide * wide, axis=0, keepdims=True)
    extra = jnp.concatenate(
        [*pieces(square), jnp.ones((3, count), F32), jnp.zeros((EXTRA - 6, count), F32)], axis=0
    )
    return jnp.concatenate([-2.0 * wide, extra], axis=0).T.astype(BF)


def right_extra(points):
    count = points.shape[1]
    return jnp.concatenate(
        [jnp.ones((3, count), F32), *pieces(square_rows(points)), jnp.zeros((EXTRA - 6, count), F32)],
        axis=0,
    ).astype(BF)


def kernel_of(left, right, depth):
    distance = jnp.dot(left, right, preferred_element_type=F32)
    return jnp.exp2(distance * (-0.5 * math.log2(math.e) / depth))


def skeleton_body(pick_ref, points_ref, residual_ref, block_ref, left_ref):
    depth, count = points_ref.shape
    rank = pick_ref.shape[1]
    points = points_ref[...]
    onehot = (lax.broadcasted_iota(jnp.int32, (count, rank), 0) == pick_ref[...]).astype(F32).astype(BF)
    chosen = jnp.dot(points, onehot, preferred_element_type=F32).astype(BF)
    right = jnp.concatenate([points, right_extra(points)], axis=0)
    tile = kernel_of(left_block(chosen), right, depth).astype(BF)
    weights = lax.dot_general(
        residual_ref[...].astype(BF), tile, NT, preferred_element_type=F32
    ) * (1.0 / math.sqrt(count))
    block = jnp.concatenate([chosen, weights.astype(BF)], axis=0)
    for copy in range(block_ref.shape[0]):
        block_ref[copy] = block
    left_ref[...] = left_block(points)


def tree_nodes(depth, upper_ref, tree_ref, nodes):
    rank = upper_ref.shape[1]
    lanes = lax.broadcasted_iota(jnp.int32, (2 * rank, rank), 0)
    both = [jnp.concatenate([tree_ref[2 * n + 1], tree_ref[2 * n + 2]], axis=1) for n in nodes]
    picks = [(lanes == upper_ref[pl.ds(n, 1), :]).astype(F32).astype(BF) for n in nodes]
    chosen = [
        jnp.dot(b[:depth], pick, preferred_element_type=F32).astype(BF) for b, pick in zip(both, picks)
    ]
    left = [left_block(points) for points in chosen]
    tiles = [kernel_of(l, b[: depth + EXTRA], depth).astype(BF) for l, b in zip(left, both)]
    ones = jnp.ones((EXTRA, 2 * rank), F32).astype(BF)
    values = [jnp.concatenate([b[depth + EXTRA :], ones], axis=0) for b in both]
    sums = [
        lax.dot_general(v, tile, NT, preferred_element_type=F32) for v, tile in zip(values, tiles)
    ]
    width = values[0].shape[0] - EXTRA
    weights = [(s[:width] / s[width : width + 1]).astype(BF) for s in sums]
    blocks = [
        jnp.concatenate([points, right_extra(points), w], axis=0)
        for points, w in zip(chosen, weights)
    ]
    for node, block in zip(nodes, blocks):
        tree_ref[node] = block


def tree_body(leaf_dev, depth, far_ref, upper_ref, left_ref, own_ref, *refs):
    part_refs, out_ref, tree_ref, acc = refs[:-3], refs[-3], refs[-2], refs[-1]
    row_total = len(part_refs)
    column_total = part_refs[0].shape[0]
    low = row_total * column_total - 1
    mine = lax.axis_index("gx")
    for slot, part_ref in enumerate(part_refs):
        first = low + lax.bitwise_xor(mine, slot) * column_total
        blocks = [part_ref[column] for column in range(column_total)]
        extras = [right_extra(block[:depth]) for block in blocks]
        for column, (block, extra) in enumerate(zip(blocks, extras)):
            tree_ref[first + column, :depth] = block[:depth]
            tree_ref[first + column, depth : depth + EXTRA] = extra
            tree_ref[first + column, depth + EXTRA :] = block[depth:]
    while low:
        low = (low - 1) // 2
        count = low + 1
        size = min(count, GROUP)

        def level(step, carry, low=low, size=size):
            tree_nodes(depth, upper_ref, tree_ref, [low + step * size + k for k in range(size)])
            return carry

        if count == size:
            level(0, 0)
        else:
            lax.fori_loop(0, count // size, level, 0)

    leaf = left_ref.shape[0] // leaf_dev
    rank = tree_ref.shape[2]
    far = far_ref.shape[1]
    for at in range(leaf_dev):
        where = slice(at * leaf, (at + 1) * leaf)
        own = own_ref[:, where]
        right = jnp.concatenate([own[:depth], right_extra(own[:depth])], axis=0)
        tile = kernel_of(left_ref[where], right, depth).astype(BF)
        acc[...] = lax.dot_general(tile, own[depth:], NT, preferred_element_type=F32) * (
            rank / math.sqrt(leaf)
        )

        def step(group, carry, at=at, where=where):
            nodes = [tree_ref[far_ref[at, 4 * group + k]] for k in range(4)]
            both = jnp.concatenate(nodes, axis=1)
            tile = kernel_of(left_ref[where], both[: depth + EXTRA], depth).astype(BF)
            acc[...] += lax.dot_general(tile, both[depth + EXTRA :], NT, preferred_element_type=F32)
            return carry

        lax.fori_loop(0, far // 4, step, 0)
        out_ref[:, where] = acc[...].T * (1.0 / rank)


def near_body(leaf_dev, depth, near_ref, left_ref, part_ref, residual_ref, *refs):
    block_refs = refs[:-5]
    image_ref, small_ref, held, sems, acc = refs[-5:]
    leaf = left_ref.shape[0] // leaf_dev
    near = near_ref.shape[1]
    mine = lax.axis_index("gy")
    columns = len(block_refs) + 1
    total = leaf_dev * near
    for request in range(total):
        wanted = near_ref[request // near, request % near]
        slot = lax.bitwise_xor(lax.rem(wanted // leaf_dev, columns), mine)
        inner = lax.rem(wanted, leaf_dev)
        for at, block_ref in enumerate(block_refs):

            @pl.when(slot == at + 1)
            def _(block_ref=block_ref, inner=inner, request=request):
                source = block_ref.at[:, pl.ds(pl.multiple_of(inner * leaf, leaf), leaf)]
                pltpu.make_async_copy(source, held.at[request], sems.at[request]).start()

    for at in range(leaf_dev):
        acc[...] = jnp.zeros_like(acc)

        def step(place, carry, at=at):
            request = at * near + place
            pltpu.make_async_copy(
                block_refs[0].at[:, :leaf], held.at[request], sems.at[request]
            ).wait()
            block = held[request]
            right = jnp.concatenate([block[:depth], right_extra(block[:depth])], axis=0)
            tile = kernel_of(left_ref[at * leaf : (at + 1) * leaf], right, depth).astype(BF)
            acc[...] += lax.dot_general(tile, block[depth:], NT, preferred_element_type=F32)
            return carry

        lax.fori_loop(0, near, step, 0)
        where = slice(at * leaf, (at + 1) * leaf)
        image_ref[:, where] = (
            LAMBDA_RIDGE * residual_ref[:, where]
            + part_ref[:, where]
            + acc[...].T * (1.0 / math.sqrt(leaf))
        )
    image = image_ref[...]
    gram = lax.dot_general(image, image, NT, precision=FULL, preferred_element_type=F32)
    cross = lax.dot_general(image, residual_ref[...], NT, precision=FULL, preferred_element_type=F32)
    half = gram.shape[0] // 2
    packed = jnp.concatenate([gram[:half], gram[half:], cross[:half], cross[half:]], axis=1)

    def copy(at, carry):
        small_ref[at] = packed
        return carry

    lax.fori_loop(0, small_ref.shape[0], copy, 0, unroll=8)


def solve_body(small_ref, solution_ref, residual_ref, image_ref, solution_out, residual_out):
    order = solution_ref.shape[0]
    packed = small_ref[0]
    for at in range(1, small_ref.shape[0]):
        packed = packed + small_ref[at]
    gram = jnp.concatenate([packed[:, :order], packed[:, order : 2 * order]], axis=0)
    cross = jnp.concatenate([packed[:, 2 * order : 3 * order], packed[:, 3 * order :]], axis=0)
    work = jnp.concatenate([gram, cross], axis=1)
    rows = lax.broadcasted_iota(jnp.int32, (order, 1), 0)
    for column in range(order):
        row = work[column : column + 1]
        inverse = 1.0 / jnp.sqrt(row[:, column : column + 1])
        factor = jnp.where(rows == column, 0.0, work[:, column : column + 1] * inverse)
        work = work - factor * (row * inverse)
    eye = (rows == lax.broadcasted_iota(jnp.int32, (order, order), 1)).astype(F32)
    diagonal = jnp.sum(work[:, :order] * eye, axis=1, keepdims=True)
    coeffs = (work[:, order:] / diagonal).T
    solution_out[...] = solution_ref[...] + jnp.dot(coeffs, residual_ref[...], precision=FULL, preferred_element_type=F32)
    residual_out[...] = residual_ref[...] - jnp.dot(coeffs, image_ref[...], precision=FULL, preferred_element_type=F32)


def step_of(points, solution, residual, near_leaves, node_skeleton, upper_skeleton, far_nodes):
    row_total = lax.axis_size("gx")
    column_total = lax.axis_size("gy")
    device_total = row_total * column_total
    leaf_dev = near_leaves.shape[0]
    near = near_leaves.shape[1]
    count, depth = points.shape
    width = residual.shape[1]
    leaf = count // leaf_dev
    rank = node_skeleton.shape[1]
    points_t = points.T
    residual_t = residual.T
    solution_t = solution.T
    near_block = jnp.concatenate([points_t, residual_t.astype(BF)], axis=0)
    top = column_total // 2
    near_blocks = {}

    def send(step, block):
        return lax.ppermute(block, "gy", [(i, i ^ step) for i in range(column_total)])

    near_blocks[top] = send(top, near_block)
    for step in [*range(top + 2, column_total, 2), *range(1, top)]:
        near_blocks[step] = send(step, near_block)
    if top > 1:
        for step in range(top, column_total, 2):
            near_blocks[step + 1] = send(1, near_blocks[step])
    deep = depth + EXTRA

    blocks, left = pl.pallas_call(
        skeleton_body,
        out_shape=(
            jax.ShapeDtypeStruct((column_total, depth + width, rank), BF),
            jax.ShapeDtypeStruct((count, deep), BF),
        ),
        in_specs=vmem(3),
        out_specs=tuple(vmem(2)),
        compiler_params=pltpu.CompilerParams(vmem_limit_bytes=GRANT),
    name="skeleton",
    )(node_skeleton, points_t, residual_t)
    mine = lax.all_to_all(blocks, "gy", 0, 0)
    parts = {0: mine}
    step = row_total // 2
    while step:
        swap = [(i, i ^ step) for i in range(row_total)]
        parts.update({slot ^ step: lax.ppermute(part, "gx", swap) for slot, part in parts.items()})
        step //= 2
    parts = [parts[slot] for slot in range(row_total)]
    partial_t = pl.pallas_call(
        functools.partial(tree_body, leaf_dev, depth),
        out_shape=jax.ShapeDtypeStruct((width, count), F32),
        in_specs=[pl.BlockSpec(memory_space=pltpu.SMEM), *vmem(3 + row_total)],
        out_specs=vmem(1)[0],
        scratch_shapes=[
            pltpu.VMEM((2 * device_total - 1, deep + width, rank), BF),
            pltpu.VMEM((leaf, width), F32),
        ],
        compiler_params=pltpu.CompilerParams(vmem_limit_bytes=GRANT),
    name="tree",
    )(far_nodes, upper_skeleton, left, near_block, *parts)
    image_t, small = pl.pallas_call(
        functools.partial(near_body, leaf_dev, depth),
        out_shape=(
            jax.ShapeDtypeStruct((width, count), F32),
            jax.ShapeDtypeStruct((device_total, width // 2, 4 * width), F32),
        ),
        in_specs=[
            pl.BlockSpec(memory_space=pltpu.SMEM),
            *vmem(3 + column_total - 1),
        ],
        out_specs=tuple(vmem(2)),
        scratch_shapes=[
            pltpu.VMEM((leaf_dev * near, depth + width, leaf), BF),
            pltpu.SemaphoreType.DMA((leaf_dev * near,)),
            pltpu.VMEM((leaf, width), F32),
        ],
        compiler_params=pltpu.CompilerParams(vmem_limit_bytes=GRANT),
        name="near",
    )(near_leaves, left, partial_t, residual_t, *[near_blocks[step] for step in range(1, column_total)])
    small = lax.all_to_all(small, ("gx", "gy"), 0, 0)
    solution_next, residual_next = pl.pallas_call(
        solve_body,
        out_shape=(jax.ShapeDtypeStruct((width, count), F32),) * 2,
        in_specs=vmem(4),
        out_specs=tuple(vmem(2)),
        compiler_params=pltpu.CompilerParams(vmem_limit_bytes=GRANT),
        name="solve",
    )(small, solution_t, residual_t, image_t)
    return (solution_next.T, residual_next.T, image_t.T)


def solution(mesh):
    split = P(("gx", "gy"), None)
    return jax.shard_map(
        step_of,
        mesh=mesh,
        in_specs=(split, split, split, split, split, P(), split),
        out_specs=(split, split, split),
        check_vma=False,
    )
```

```python
import functools
import math

import jax
import jax.numpy as jnp
from jax import lax
from jax.experimental import pallas as pl
from jax.experimental.pallas import tpu as pltpu
from jax.sharding import PartitionSpec as P


LAMBDA_RIDGE = 1.0
FULL = lax.Precision.HIGHEST
BF = jnp.bfloat16
F32 = jnp.float32
EXTRA = 16
GROUP = 16
GRANT = 24 * 2**20
NT = (((1,), (1,)), ((), ()))


def vmem(count):
    return [pl.BlockSpec(memory_space=pltpu.VMEM)] * count


def pieces(value):
    high = value.astype(BF).astype(F32)
    rest = value - high
    middle = rest.astype(BF).astype(F32)
    return high, middle, (rest - middle).astype(BF).astype(F32)


def square_rows(points):
    wide = points.astype(F32)
    return jnp.sum(wide * wide, axis=0, keepdims=True)


def left_block(points):
    count = points.shape[1]
    wide = points.astype(F32)
    square = jnp.sum(wide * wide, axis=0, keepdims=True)
    extra = jnp.concatenate(
        [*pieces(square), jnp.ones((3, count), F32), jnp.zeros((EXTRA - 6, count), F32)], axis=0
    )
    return jnp.concatenate([-2.0 * wide, extra], axis=0).T.astype(BF)


def right_extra(points):
    count = points.shape[1]
    return jnp.concatenate(
        [jnp.ones((3, count), F32), *pieces(square_rows(points)), jnp.zeros((EXTRA - 6, count), F32)],
        axis=0,
    ).astype(BF)


def kernel_of(left, right, depth):
    distance = jnp.dot(left, right, preferred_element_type=F32)
    return jnp.exp2(distance * (-0.5 * math.log2(math.e) / depth))


def fields(sources, right, depth):
    left = [left_block(source[:depth]) for source in sources]
    tiles = [kernel_of(block, right, depth).astype(BF) for block in left]
    sums = [
        jnp.dot(source[depth:], tile, preferred_element_type=F32)
        for source, tile in zip(sources, tiles)
    ]
    return sum(sums[1:], sums[0])


def skeleton_body(pick_ref, points_ref, residual_ref, block_ref, right_ref):
    depth, count = points_ref.shape
    rank = pick_ref.shape[1]
    points = points_ref[...]
    onehot = (lax.broadcasted_iota(jnp.int32, (count, rank), 0) == pick_ref[...]).astype(F32).astype(BF)
    chosen = jnp.dot(points, onehot, preferred_element_type=F32).astype(BF)
    right = jnp.concatenate([points, right_extra(points)], axis=0)
    tile = kernel_of(left_block(chosen), right, depth).astype(BF)
    weights = lax.dot_general(
        residual_ref[...].astype(BF), tile, NT, preferred_element_type=F32
    ) * (1.0 / math.sqrt(count))
    block = jnp.concatenate([chosen, weights.astype(BF)], axis=0)
    for copy in range(block_ref.shape[0]):
        block_ref[copy] = block
    right_ref[...] = right


def tree_nodes(depth, upper_ref, tree_ref, nodes):
    rank = upper_ref.shape[1]
    lanes = lax.broadcasted_iota(jnp.int32, (2 * rank, rank), 0)
    both = [jnp.concatenate([tree_ref[2 * n + 1], tree_ref[2 * n + 2]], axis=1) for n in nodes]
    picks = [(lanes == upper_ref[pl.ds(n, 1), :]).astype(F32).astype(BF) for n in nodes]
    chosen = [
        jnp.dot(b[:depth], pick, preferred_element_type=F32).astype(BF) for b, pick in zip(both, picks)
    ]
    left = [left_block(points) for points in chosen]
    tiles = [kernel_of(l, b[: depth + EXTRA], depth).astype(BF) for l, b in zip(left, both)]
    ones = jnp.ones((EXTRA, 2 * rank), F32).astype(BF)
    values = [jnp.concatenate([b[depth + EXTRA :], ones], axis=0) for b in both]
    sums = [
        lax.dot_general(v, tile, NT, preferred_element_type=F32) for v, tile in zip(values, tiles)
    ]
    width = values[0].shape[0] - EXTRA
    weights = [(s[:width] / s[width : width + 1]).astype(BF) for s in sums]
    blocks = [
        jnp.concatenate([points, right_extra(points), w], axis=0)
        for points, w in zip(chosen, weights)
    ]
    for node, block in zip(nodes, blocks):
        tree_ref[node] = block


def tree_body(leaf_dev, depth, far_ref, upper_ref, right_ref, own_ref, *refs):
    part_refs, out_ref, tree_ref = refs[:-2], refs[-2], refs[-1]
    row_total = len(part_refs)
    column_total = part_refs[0].shape[0]
    low = row_total * column_total - 1
    mine = lax.axis_index("gx")
    for slot, part_ref in enumerate(part_refs):
        first = low + lax.bitwise_xor(mine, slot) * column_total
        blocks = [part_ref[column] for column in range(column_total)]
        extras = [right_extra(block[:depth]) for block in blocks]
        for column, (block, extra) in enumerate(zip(blocks, extras)):
            tree_ref[first + column, :depth] = block[:depth]
            tree_ref[first + column, depth : depth + EXTRA] = extra
            tree_ref[first + column, depth + EXTRA :] = block[depth:]
    while low:
        low = (low - 1) // 2
        count = low + 1
        size = min(count, GROUP)

        def level(step, carry, low=low, size=size):
            tree_nodes(depth, upper_ref, tree_ref, [low + step * size + k for k in range(size)])
            return carry

        if count == size:
            level(0, 0)
        else:
            lax.fori_loop(0, count // size, level, 0)

    leaf = right_ref.shape[1] // leaf_dev
    rank = tree_ref.shape[2]
    far = far_ref.shape[1]
    each = leaf // rank
    for at in range(leaf_dev):
        where = slice(at * leaf, (at + 1) * leaf)
        sources = []
        for first in range(0, far, each):
            both = jnp.concatenate([tree_ref[far_ref[at, first + k]] for k in range(each)], axis=1)
            sources.append(jnp.concatenate([both[:depth], both[depth + EXTRA :]], axis=0))
        right = right_ref[:, where]
        out_ref[:, where] = fields(sources, right, depth) * (1.0 / rank) + fields(
            [own_ref[:, where]], right, depth
        ) * (1.0 / math.sqrt(leaf))


def near_body(leaf_dev, depth, near_ref, right_ref, part_ref, residual_ref, *refs):
    block_refs = refs[:-4]
    image_ref, small_ref, held, sems = refs[-4:]
    leaf = right_ref.shape[1] // leaf_dev
    near = near_ref.shape[1]
    mine = lax.axis_index("gy")
    columns = len(block_refs) + 1
    total = leaf_dev * near
    for request in range(total):
        wanted = near_ref[request // near, request % near]
        slot = lax.bitwise_xor(lax.rem(wanted // leaf_dev, columns), mine)
        inner = lax.rem(wanted, leaf_dev)
        for at, block_ref in enumerate(block_refs):

            @pl.when(slot == at + 1)
            def _(block_ref=block_ref, inner=inner, request=request):
                source = block_ref.at[:, pl.ds(pl.multiple_of(inner * leaf, leaf), leaf)]
                pltpu.make_async_copy(source, held.at[request], sems.at[request]).start()

    for at in range(leaf_dev):
        requests = range(at * near, (at + 1) * near)
        for request in requests:
            pltpu.make_async_copy(
                block_refs[0].at[:, :leaf], held.at[request], sems.at[request]
            ).wait()
        where = slice(at * leaf, (at + 1) * leaf)
        total = fields([held[request] for request in requests], right_ref[:, where], depth)
        image_ref[:, where] = (
            LAMBDA_RIDGE * residual_ref[:, where]
            + part_ref[:, where]
            + total * (1.0 / math.sqrt(leaf))
        )
    image = image_ref[...]
    gram = lax.dot_general(image, image, NT, precision=FULL, preferred_element_type=F32)
    cross = lax.dot_general(image, residual_ref[...], NT, precision=FULL, preferred_element_type=F32)
    half = gram.shape[0] // 2
    packed = jnp.concatenate([gram[:half], gram[half:], cross[:half], cross[half:]], axis=1)

    def copy(at, carry):
        small_ref[at] = packed
        return carry

    lax.fori_loop(0, small_ref.shape[0], copy, 0, unroll=8)


def solve_body(small_ref, solution_ref, residual_ref, image_ref, solution_out, residual_out):
    order = solution_ref.shape[0]
    packed = small_ref[0]
    for at in range(1, small_ref.shape[0]):
        packed = packed + small_ref[at]
    gram = jnp.concatenate([packed[:, :order], packed[:, order : 2 * order]], axis=0)
    cross = jnp.concatenate([packed[:, 2 * order : 3 * order], packed[:, 3 * order :]], axis=0)
    rows = lax.broadcasted_iota(jnp.int32, (order, 1), 0)
    eye = (rows == lax.broadcasted_iota(jnp.int32, (order, order), 1)).astype(F32)
    down = lax.rsqrt(jnp.sum(gram * eye, axis=1, keepdims=True))
    across = lax.rsqrt(jnp.sum(gram * eye, axis=0, keepdims=True))
    work = jnp.concatenate([gram * down * across, cross * down], axis=1)
    inverses = []
    for first in range(0, order, 2):
        upper, lower = work[first : first + 1], work[first + 1 : first + 2]
        a, b, c = upper[:, first : first + 1], upper[:, first + 1 : first + 2], lower[:, first + 1 : first + 2]
        scale = 1.0 / (a * c - b * b)
        inverse = (c * scale, -b * scale, a * scale)
        inverses.append(inverse)
        inside = (rows == first) | (rows == first + 1)
        left = jnp.where(inside, 0.0, work[:, first : first + 1])
        right = jnp.where(inside, 0.0, work[:, first + 1 : first + 2])
        work = (
            work
            - (left * inverse[0] + right * inverse[1]) * upper
            - (left * inverse[1] + right * inverse[2]) * lower
        )
    found = []
    for first, inverse in zip(range(0, order, 2), inverses):
        upper, lower = work[first : first + 1, order:], work[first + 1 : first + 2, order:]
        found.append(inverse[0] * upper + inverse[1] * lower)
        found.append(inverse[1] * upper + inverse[2] * lower)
    coeffs = (jnp.concatenate(found, axis=0) * down).T
    solution_out[...] = solution_ref[...] + jnp.dot(coeffs, residual_ref[...], precision=FULL, preferred_element_type=F32)
    residual_out[...] = residual_ref[...] - jnp.dot(coeffs, image_ref[...], precision=FULL, preferred_element_type=F32)


def step_of(points, solution, residual, near_leaves, node_skeleton, upper_skeleton, far_nodes):
    row_total = lax.axis_size("gx")
    column_total = lax.axis_size("gy")
    device_total = row_total * column_total
    leaf_dev = near_leaves.shape[0]
    near = near_leaves.shape[1]
    count, depth = points.shape
    width = residual.shape[1]
    leaf = count // leaf_dev
    rank = node_skeleton.shape[1]
    points_t = points.T
    residual_t = residual.T
    solution_t = solution.T
    near_block = jnp.concatenate([points_t, residual_t.astype(BF)], axis=0)
    top = column_total // 2
    near_blocks = {}

    def send(step, block):
        return lax.ppermute(block, "gy", [(i, i ^ step) for i in range(column_total)])

    near_blocks[top] = send(top, near_block)
    for step in [*range(top + 2, column_total, 2), *range(1, top)]:
        near_blocks[step] = send(step, near_block)
    if top > 1:
        for step in range(top, column_total, 2):
            near_blocks[step + 1] = send(1, near_blocks[step])
    deep = depth + EXTRA

    blocks, right = pl.pallas_call(
        skeleton_body,
        out_shape=(
            jax.ShapeDtypeStruct((column_total, depth + width, rank), BF),
            jax.ShapeDtypeStruct((deep, count), BF),
        ),
        in_specs=vmem(3),
        out_specs=tuple(vmem(2)),
        compiler_params=pltpu.CompilerParams(vmem_limit_bytes=GRANT),
    name="skeleton",
    )(node_skeleton, points_t, residual_t)
    mine = lax.all_to_all(blocks, "gy", 0, 0)
    parts = {0: mine}
    step = row_total // 2
    while step:
        swap = [(i, i ^ step) for i in range(row_total)]
        parts.update({slot ^ step: lax.ppermute(part, "gx", swap) for slot, part in parts.items()})
        step //= 2
    parts = [parts[slot] for slot in range(row_total)]
    partial_t = pl.pallas_call(
        functools.partial(tree_body, leaf_dev, depth),
        out_shape=jax.ShapeDtypeStruct((width, count), F32),
        in_specs=[pl.BlockSpec(memory_space=pltpu.SMEM), *vmem(3 + row_total)],
        out_specs=vmem(1)[0],
        scratch_shapes=[
            pltpu.VMEM((2 * device_total - 1, deep + width, rank), BF),
        ],
        compiler_params=pltpu.CompilerParams(vmem_limit_bytes=GRANT),
    name="tree",
    )(far_nodes, upper_skeleton, right, near_block, *parts)
    image_t, small = pl.pallas_call(
        functools.partial(near_body, leaf_dev, depth),
        out_shape=(
            jax.ShapeDtypeStruct((width, count), F32),
            jax.ShapeDtypeStruct((device_total, width // 2, 4 * width), F32),
        ),
        in_specs=[
            pl.BlockSpec(memory_space=pltpu.SMEM),
            *vmem(3 + column_total - 1),
        ],
        out_specs=tuple(vmem(2)),
        scratch_shapes=[
            pltpu.VMEM((leaf_dev * near, depth + width, leaf), BF),
            pltpu.SemaphoreType.DMA((leaf_dev * near,)),
        ],
        compiler_params=pltpu.CompilerParams(vmem_limit_bytes=GRANT),
        name="near",
    )(near_leaves, right, partial_t, residual_t, *[near_blocks[step] for step in range(1, column_total)])
    small = lax.all_to_all(small, ("gx", "gy"), 0, 0)
    solution_next, residual_next = pl.pallas_call(
        solve_body,
        out_shape=(jax.ShapeDtypeStruct((width, count), F32),) * 2,
        in_specs=vmem(4),
        out_specs=tuple(vmem(2)),
        compiler_params=pltpu.CompilerParams(vmem_limit_bytes=GRANT),
        name="solve",
    )(small, solution_t, residual_t, image_t)
    return (solution_next.T, residual_next.T, image_t.T)


def solution(mesh):
    split = P(("gx", "gy"), None)
    return jax.shard_map(
        step_of,
        mesh=mesh,
        in_specs=(split, split, split, split, split, P(), split),
        out_specs=(split, split, split),
        check_vma=False,
    )
```

```python
import functools
import math

import jax
import jax.numpy as jnp
from jax import lax
from jax.experimental import pallas as pl
from jax.experimental.pallas import tpu as pltpu
from jax.sharding import PartitionSpec as P


LAMBDA_RIDGE = 1.0
FULL = lax.Precision.HIGHEST
BF = jnp.bfloat16
F32 = jnp.float32
EXTRA = 16
GROUP = 16
AHEAD = 4
GRANT = 24 * 2**20
NT = (((1,), (1,)), ((), ()))


def vmem(count):
    return [pl.BlockSpec(memory_space=pltpu.VMEM)] * count


def pieces(value):
    high = value.astype(BF).astype(F32)
    rest = value - high
    middle = rest.astype(BF).astype(F32)
    return high, middle, (rest - middle).astype(BF).astype(F32)


def square_rows(points):
    wide = points.astype(F32)
    return jnp.sum(wide * wide, axis=0, keepdims=True)


def left_block(points):
    count = points.shape[1]
    wide = points.astype(F32)
    square = jnp.sum(wide * wide, axis=0, keepdims=True)
    extra = jnp.concatenate(
        [*pieces(square), jnp.ones((3, count), F32), jnp.zeros((EXTRA - 6, count), F32)], axis=0
    )
    return jnp.concatenate([-2.0 * wide, extra], axis=0).T.astype(BF)


def right_extra(points):
    count = points.shape[1]
    return jnp.concatenate(
        [jnp.ones((3, count), F32), *pieces(square_rows(points)), jnp.zeros((EXTRA - 6, count), F32)],
        axis=0,
    ).astype(BF)


def kernel_of(left, right, depth):
    distance = jnp.dot(left, right, preferred_element_type=F32)
    return jnp.exp2(distance * (-0.5 * math.log2(math.e) / depth))


def fields(sources, right, depth):
    left = [left_block(source[:depth]) for source in sources]
    tiles = [kernel_of(block, right, depth).astype(BF) for block in left]
    sums = [
        jnp.dot(source[depth:], tile, preferred_element_type=F32)
        for source, tile in zip(sources, tiles)
    ]
    return sum(sums[1:], sums[0])


def skeleton_body(pick_ref, points_ref, residual_ref, block_ref, right_ref):
    depth, count = points_ref.shape
    rank = pick_ref.shape[1]
    points = points_ref[...]
    onehot = (lax.broadcasted_iota(jnp.int32, (count, rank), 0) == pick_ref[...]).astype(F32).astype(BF)
    chosen = jnp.dot(points, onehot, preferred_element_type=F32).astype(BF)
    right = jnp.concatenate([points, right_extra(points)], axis=0)
    tile = kernel_of(left_block(chosen), right, depth).astype(BF)
    weights = lax.dot_general(
        residual_ref[...].astype(BF), tile, NT, preferred_element_type=F32
    ) * (1.0 / math.sqrt(count))
    block = jnp.concatenate([chosen, weights.astype(BF)], axis=0)
    for copy in range(block_ref.shape[0]):
        block_ref[copy] = block
    right_ref[...] = right


def tree_nodes(depth, upper_ref, tree_ref, nodes):
    rank = upper_ref.shape[1]
    lanes = lax.broadcasted_iota(jnp.int32, (2 * rank, rank), 0)
    both = [jnp.concatenate([tree_ref[2 * n + 1], tree_ref[2 * n + 2]], axis=1) for n in nodes]
    picks = [(lanes == upper_ref[pl.ds(n, 1), :]).astype(F32).astype(BF) for n in nodes]
    chosen = [
        jnp.dot(b[:depth], pick, preferred_element_type=F32).astype(BF) for b, pick in zip(both, picks)
    ]
    left = [left_block(points) for points in chosen]
    tiles = [kernel_of(l, b[: depth + EXTRA], depth).astype(BF) for l, b in zip(left, both)]
    ones = jnp.ones((EXTRA, 2 * rank), F32).astype(BF)
    values = [jnp.concatenate([b[depth + EXTRA :], ones], axis=0) for b in both]
    sums = [
        lax.dot_general(v, tile, NT, preferred_element_type=F32) for v, tile in zip(values, tiles)
    ]
    width = values[0].shape[0] - EXTRA
    weights = [(s[:width] / s[width : width + 1]).astype(BF) for s in sums]
    blocks = [
        jnp.concatenate([points, right_extra(points), w], axis=0)
        for points, w in zip(chosen, weights)
    ]
    for node, block in zip(nodes, blocks):
        tree_ref[node] = block


def tree_body(leaf_dev, depth, far_ref, upper_ref, right_ref, own_ref, *refs):
    part_refs, out_ref, tree_ref = refs[:-2], refs[-2], refs[-1]
    row_total = len(part_refs)
    column_total = part_refs[0].shape[0]
    low = row_total * column_total - 1
    mine = lax.axis_index("gx")
    for slot, part_ref in enumerate(part_refs):
        first = low + lax.bitwise_xor(mine, slot) * column_total
        blocks = [part_ref[column] for column in range(column_total)]
        extras = [right_extra(block[:depth]) for block in blocks]
        for column, (block, extra) in enumerate(zip(blocks, extras)):
            tree_ref[first + column, :depth] = block[:depth]
            tree_ref[first + column, depth : depth + EXTRA] = extra
            tree_ref[first + column, depth + EXTRA :] = block[depth:]
    while low:
        low = (low - 1) // 2
        count = low + 1
        size = min(count, GROUP)

        def level(step, carry, low=low, size=size):
            tree_nodes(depth, upper_ref, tree_ref, [low + step * size + k for k in range(size)])
            return carry

        if count == size:
            level(0, 0)
        else:
            lax.fori_loop(0, count // size, level, 0)

    leaf = right_ref.shape[1] // leaf_dev
    rank = tree_ref.shape[2]
    far = far_ref.shape[1]
    each = leaf // rank
    for at in range(leaf_dev):
        where = slice(at * leaf, (at + 1) * leaf)
        sources = []
        for first in range(0, far, each):
            both = jnp.concatenate([tree_ref[far_ref[at, first + k]] for k in range(each)], axis=1)
            sources.append(jnp.concatenate([both[:depth], both[depth + EXTRA :]], axis=0))
        right = right_ref[:, where]
        out_ref[:, where] = fields(sources, right, depth) * (1.0 / rank) + fields(
            [own_ref[:, where]], right, depth
        ) * (1.0 / math.sqrt(leaf))


def near_body(leaf_dev, depth, near_ref, right_ref, part_ref, residual_ref, *refs):
    block_refs = refs[:-4]
    image_ref, small_ref, held, sems = refs[-4:]
    leaf = right_ref.shape[1] // leaf_dev
    near = near_ref.shape[1]
    mine = lax.axis_index("gy")
    columns = len(block_refs) + 1
    total = leaf_dev * near
    for request in range(total):
        wanted = near_ref[request // near, request % near]
        slot = lax.bitwise_xor(lax.rem(wanted // leaf_dev, columns), mine)
        inner = lax.rem(wanted, leaf_dev)
        for at, block_ref in enumerate(block_refs):

            @pl.when(slot == at + 1)
            def _(block_ref=block_ref, inner=inner, request=request):
                source = block_ref.at[:, pl.ds(pl.multiple_of(inner * leaf, leaf), leaf)]
                pltpu.make_async_copy(source, held.at[request], sems.at[request]).start()

    for at in range(leaf_dev):
        requests = range(at * near, (at + 1) * near)
        for request in requests:
            pltpu.make_async_copy(
                block_refs[0].at[:, :leaf], held.at[request], sems.at[request]
            ).wait()
        where = slice(at * leaf, (at + 1) * leaf)
        total = fields([held[request] for request in requests], right_ref[:, where], depth)
        image_ref[:, where] = (
            LAMBDA_RIDGE * residual_ref[:, where]
            + part_ref[:, where]
            + total * (1.0 / math.sqrt(leaf))
        )
    image = image_ref[...]
    gram = lax.dot_general(image, image, NT, precision=FULL, preferred_element_type=F32)
    cross = lax.dot_general(image, residual_ref[...], NT, precision=FULL, preferred_element_type=F32)
    half = gram.shape[0] // 2
    packed = jnp.concatenate([gram[:half], gram[half:], cross[:half], cross[half:]], axis=1)

    def copy(at, carry):
        small_ref[at] = packed
        return carry

    lax.fori_loop(0, small_ref.shape[0], copy, 0, unroll=8)


def solve_body(small_ref, solution_ref, residual_ref, image_ref, solution_out, residual_out):
    order = solution_ref.shape[0]
    packed = small_ref[0]
    for at in range(1, small_ref.shape[0]):
        packed = packed + small_ref[at]
    gram = jnp.concatenate([packed[:, :order], packed[:, order : 2 * order]], axis=0)
    cross = jnp.concatenate([packed[:, 2 * order : 3 * order], packed[:, 3 * order :]], axis=0)
    work = jnp.concatenate([gram, cross], axis=1)
    rows = lax.broadcasted_iota(jnp.int32, (order, 1), 0)

    def wide(column):
        return jnp.broadcast_to(work[:, column : column + 1], work.shape)

    ahead = [wide(column) for column in range(min(order, AHEAD + 1))]
    for column in range(order):
        pivots = ahead.pop(0)
        inverse = 1.0 / pivots[column : column + 1]
        factor = jnp.where(rows == column, 0.0, pivots)
        ahead = [later - factor * (later[column : column + 1] * inverse) for later in ahead]
        work = work - factor * (work[column : column + 1] * inverse)
        if column + AHEAD + 1 < order:
            ahead.append(wide(column + AHEAD + 1))
    eye = (rows == lax.broadcasted_iota(jnp.int32, (order, order), 1)).astype(F32)
    diagonal = jnp.sum(work[:, :order] * eye, axis=1, keepdims=True)
    coeffs = (work[:, order:] / diagonal).T
    solution_out[...] = solution_ref[...] + jnp.dot(coeffs, residual_ref[...], precision=FULL, preferred_element_type=F32)
    residual_out[...] = residual_ref[...] - jnp.dot(coeffs, image_ref[...], precision=FULL, preferred_element_type=F32)


def step_of(points, solution, residual, near_leaves, node_skeleton, upper_skeleton, far_nodes):
    row_total = lax.axis_size("gx")
    column_total = lax.axis_size("gy")
    device_total = row_total * column_total
    leaf_dev = near_leaves.shape[0]
    near = near_leaves.shape[1]
    count, depth = points.shape
    width = residual.shape[1]
    leaf = count // leaf_dev
    rank = node_skeleton.shape[1]
    points_t = points.T
    residual_t = residual.T
    solution_t = solution.T
    near_block = jnp.concatenate([points_t, residual_t.astype(BF)], axis=0)
    top = column_total // 2
    near_blocks = {}

    def send(step, block):
        return lax.ppermute(block, "gy", [(i, i ^ step) for i in range(column_total)])

    for step in [*range(top, column_total, 2), *range(1, min(top, 2))]:
        near_blocks[step] = send(step, near_block)
    for step in range(2, top):
        near_blocks[step] = send(step, near_block)
    if top > 1:
        for step in range(top, column_total, 2):
            near_blocks[step + 1] = send(1, near_blocks[step])
    deep = depth + EXTRA

    blocks, right = pl.pallas_call(
        skeleton_body,
        out_shape=(
            jax.ShapeDtypeStruct((column_total, depth + width, rank), BF),
            jax.ShapeDtypeStruct((deep, count), BF),
        ),
        in_specs=vmem(3),
        out_specs=tuple(vmem(2)),
        compiler_params=pltpu.CompilerParams(vmem_limit_bytes=GRANT),
    name="skeleton",
    )(node_skeleton, points_t, residual_t)
    mine = lax.all_to_all(blocks, "gy", 0, 0)
    parts = {0: mine}
    step = row_total // 2
    while step:
        swap = [(i, i ^ step) for i in range(row_total)]
        parts.update({slot ^ step: lax.ppermute(part, "gx", swap) for slot, part in parts.items()})
        step //= 2
    parts = [parts[slot] for slot in range(row_total)]
    partial_t = pl.pallas_call(
        functools.partial(tree_body, leaf_dev, depth),
        out_shape=jax.ShapeDtypeStruct((width, count), F32),
        in_specs=[pl.BlockSpec(memory_space=pltpu.SMEM), *vmem(3 + row_total)],
        out_specs=vmem(1)[0],
        scratch_shapes=[
            pltpu.VMEM((2 * device_total - 1, deep + width, rank), BF),
        ],
        compiler_params=pltpu.CompilerParams(vmem_limit_bytes=GRANT),
    name="tree",
    )(far_nodes, upper_skeleton, right, near_block, *parts)
    image_t, small = pl.pallas_call(
        functools.partial(near_body, leaf_dev, depth),
        out_shape=(
            jax.ShapeDtypeStruct((width, count), F32),
            jax.ShapeDtypeStruct((device_total, width // 2, 4 * width), F32),
        ),
        in_specs=[
            pl.BlockSpec(memory_space=pltpu.SMEM),
            *vmem(3 + column_total - 1),
        ],
        out_specs=tuple(vmem(2)),
        scratch_shapes=[
            pltpu.VMEM((leaf_dev * near, depth + width, leaf), BF),
            pltpu.SemaphoreType.DMA((leaf_dev * near,)),
        ],
        compiler_params=pltpu.CompilerParams(vmem_limit_bytes=GRANT),
        name="near",
    )(near_leaves, right, partial_t, residual_t, *[near_blocks[step] for step in range(1, column_total)])
    small = lax.all_to_all(small, ("gx", "gy"), 0, 0)
    solution_next, residual_next = pl.pallas_call(
        solve_body,
        out_shape=(jax.ShapeDtypeStruct((width, count), F32),) * 2,
        in_specs=vmem(4),
        out_specs=tuple(vmem(2)),
        compiler_params=pltpu.CompilerParams(vmem_limit_bytes=GRANT),
        name="solve",
    )(small, solution_t, residual_t, image_t)
    return (solution_next.T, residual_next.T, image_t.T)


def solution(mesh):
    split = P(("gx", "gy"), None)
    return jax.shard_map(
        step_of,
        mesh=mesh,
        in_specs=(split, split, split, split, split, P(), split),
        out_specs=(split, split, split),
        check_vma=False,
    )
```

```python
import functools
import math

import jax
import jax.numpy as jnp
from jax import lax
from jax.experimental import pallas as pl
from jax.experimental.pallas import tpu as pltpu
from jax.sharding import PartitionSpec as P


LAMBDA_RIDGE = 1.0
FULL = lax.Precision.HIGHEST
BF = jnp.bfloat16
F32 = jnp.float32
EXTRA = 16
GROUP = 16
AHEAD = 4
GRANT = 24 * 2**20
NT = (((1,), (1,)), ((), ()))


def vmem(count):
    return [pl.BlockSpec(memory_space=pltpu.VMEM)] * count


def pieces(value):
    high = value.astype(BF).astype(F32)
    rest = value - high
    middle = rest.astype(BF).astype(F32)
    return high, middle, (rest - middle).astype(BF).astype(F32)


def square_rows(points):
    wide = points.astype(F32)
    return jnp.sum(wide * wide, axis=0, keepdims=True)


def left_block(points):
    count = points.shape[1]
    wide = points.astype(F32)
    square = jnp.sum(wide * wide, axis=0, keepdims=True)
    extra = jnp.concatenate(
        [*pieces(square), jnp.ones((3, count), F32), jnp.zeros((EXTRA - 6, count), F32)], axis=0
    )
    return jnp.concatenate([-2.0 * wide, extra], axis=0).T.astype(BF)


def right_extra(points):
    count = points.shape[1]
    return jnp.concatenate(
        [jnp.ones((3, count), F32), *pieces(square_rows(points)), jnp.zeros((EXTRA - 6, count), F32)],
        axis=0,
    ).astype(BF)


def kernel_of(left, right, depth):
    distance = jnp.dot(left, right, preferred_element_type=F32)
    return jnp.exp2(distance * (-0.5 * math.log2(math.e) / depth))


def fields(sources, right, depth):
    left = [left_block(source[:depth]) for source in sources]
    tiles = [kernel_of(block, right, depth).astype(BF) for block in left]
    sums = [
        jnp.dot(source[depth:], tile, preferred_element_type=F32)
        for source, tile in zip(sources, tiles)
    ]
    return sum(sums[1:], sums[0])


def skeleton_body(pick_ref, points_ref, residual_ref, block_ref, right_ref):
    depth, count = points_ref.shape
    rank = pick_ref.shape[1]
    points = points_ref[...]
    onehot = (lax.broadcasted_iota(jnp.int32, (count, rank), 0) == pick_ref[...]).astype(F32).astype(BF)
    chosen = jnp.dot(points, onehot, preferred_element_type=F32).astype(BF)
    right = jnp.concatenate([points, right_extra(points)], axis=0)
    tile = kernel_of(left_block(chosen), right, depth).astype(BF)
    weights = lax.dot_general(
        residual_ref[...].astype(BF), tile, NT, preferred_element_type=F32
    ) * (1.0 / math.sqrt(count))
    block = jnp.concatenate([chosen, weights.astype(BF)], axis=0)
    for copy in range(block_ref.shape[0]):
        block_ref[copy] = block
    right_ref[...] = right


def tree_nodes(depth, upper_ref, tree_ref, nodes):
    rank = upper_ref.shape[1]
    lanes = lax.broadcasted_iota(jnp.int32, (2 * rank, rank), 0)
    both = [jnp.concatenate([tree_ref[2 * n + 1], tree_ref[2 * n + 2]], axis=1) for n in nodes]
    picks = [(lanes == upper_ref[pl.ds(n, 1), :]).astype(F32).astype(BF) for n in nodes]
    chosen = [
        jnp.dot(b[:depth], pick, preferred_element_type=F32).astype(BF) for b, pick in zip(both, picks)
    ]
    left = [left_block(points) for points in chosen]
    tiles = [kernel_of(l, b[: depth + EXTRA], depth).astype(BF) for l, b in zip(left, both)]
    ones = jnp.ones((EXTRA, 2 * rank), F32).astype(BF)
    values = [jnp.concatenate([b[depth + EXTRA :], ones], axis=0) for b in both]
    sums = [
        lax.dot_general(v, tile, NT, preferred_element_type=F32) for v, tile in zip(values, tiles)
    ]
    width = values[0].shape[0] - EXTRA
    weights = [(s[:width] / s[width : width + 1]).astype(BF) for s in sums]
    blocks = [
        jnp.concatenate([points, right_extra(points), w], axis=0)
        for points, w in zip(chosen, weights)
    ]
    for node, block in zip(nodes, blocks):
        tree_ref[node] = block


def tree_body(leaf_dev, depth, far_ref, upper_ref, right_ref, own_ref, *refs):
    part_refs, out_ref, tree_ref = refs[:-2], refs[-2], refs[-1]
    row_total = len(part_refs)
    column_total = part_refs[0].shape[0]
    low = row_total * column_total - 1
    mine = lax.axis_index("gx")
    for slot, part_ref in enumerate(part_refs):
        first = low + lax.bitwise_xor(mine, slot) * column_total
        blocks = [part_ref[column] for column in range(column_total)]
        extras = [right_extra(block[:depth]) for block in blocks]
        for column, (block, extra) in enumerate(zip(blocks, extras)):
            tree_ref[first + column, :depth] = block[:depth]
            tree_ref[first + column, depth : depth + EXTRA] = extra
            tree_ref[first + column, depth + EXTRA :] = block[depth:]
    while low:
        low = (low - 1) // 2
        count = low + 1
        size = min(count, GROUP)

        def level(step, carry, low=low, size=size):
            tree_nodes(depth, upper_ref, tree_ref, [low + step * size + k for k in range(size)])
            return carry

        if count == size:
            level(0, 0)
        else:
            lax.fori_loop(0, count // size, level, 0)

    leaf = right_ref.shape[1] // leaf_dev
    rank = tree_ref.shape[2]
    far = far_ref.shape[1]
    each = leaf // rank
    for at in range(leaf_dev):
        where = slice(at * leaf, (at + 1) * leaf)
        sources = []
        for first in range(0, far, each):
            both = jnp.concatenate([tree_ref[far_ref[at, first + k]] for k in range(each)], axis=1)
            sources.append(jnp.concatenate([both[:depth], both[depth + EXTRA :]], axis=0))
        right = right_ref[:, where]
        out_ref[:, where] = fields(sources, right, depth) * (1.0 / rank) + fields(
            [own_ref[:, where]], right, depth
        ) * (1.0 / math.sqrt(leaf))


def near_body(leaf_dev, depth, near_ref, right_ref, part_ref, residual_ref, *refs):
    block_refs = refs[:-4]
    image_ref, small_ref, held, sems = refs[-4:]
    leaf = right_ref.shape[1] // leaf_dev
    near = near_ref.shape[1]
    mine = lax.axis_index("gy")
    columns = len(block_refs) + 1
    total = leaf_dev * near
    for request in range(total):
        wanted = near_ref[request // near, request % near]
        slot = lax.bitwise_xor(lax.rem(wanted // leaf_dev, columns), mine)
        inner = lax.rem(wanted, leaf_dev)
        for at, block_ref in enumerate(block_refs):

            @pl.when(slot == at + 1)
            def _(block_ref=block_ref, inner=inner, request=request):
                source = block_ref.at[:, pl.ds(pl.multiple_of(inner * leaf, leaf), leaf)]
                pltpu.make_async_copy(source, held.at[request], sems.at[request]).start()

    for at in range(leaf_dev):
        requests = range(at * near, (at + 1) * near)
        for request in requests:
            pltpu.make_async_copy(
                block_refs[0].at[:, :leaf], held.at[request], sems.at[request]
            ).wait()
        where = slice(at * leaf, (at + 1) * leaf)
        total = fields([held[request] for request in requests], right_ref[:, where], depth)
        image_ref[:, where] = (
            LAMBDA_RIDGE * residual_ref[:, where]
            + part_ref[:, where]
            + total * (1.0 / math.sqrt(leaf))
        )
    image = image_ref[...]
    gram = lax.dot_general(image, image, NT, precision=FULL, preferred_element_type=F32)
    cross = lax.dot_general(image, residual_ref[...], NT, precision=FULL, preferred_element_type=F32)
    half = gram.shape[0] // 2
    packed = jnp.concatenate([gram[:half], gram[half:], cross[:half], cross[half:]], axis=1)

    def copy(at, carry):
        small_ref[at] = packed
        return carry

    lax.fori_loop(0, small_ref.shape[0], copy, 0, unroll=8)


def solve_body(small_ref, solution_ref, residual_ref, image_ref, solution_out, residual_out):
    order = solution_ref.shape[0]
    packed = small_ref[0]
    for at in range(1, small_ref.shape[0]):
        packed = packed + small_ref[at]
    gram = jnp.concatenate([packed[:, :order], packed[:, order : 2 * order]], axis=0)
    cross = jnp.concatenate([packed[:, 2 * order : 3 * order], packed[:, 3 * order :]], axis=0)
    work = jnp.concatenate([gram, cross], axis=1)
    rows = lax.broadcasted_iota(jnp.int32, (order, 1), 0)

    def wide(column):
        return jnp.broadcast_to(work[:, column : column + 1], work.shape)

    ahead = [wide(column) for column in range(min(order, AHEAD + 1))]
    for column in range(order):
        pivots = ahead.pop(0)
        inverse = 1.0 / pivots[column : column + 1]
        factor = jnp.where(rows == column, 0.0, pivots)
        ahead = [later - factor * (later[column : column + 1] * inverse) for later in ahead]
        work = work - factor * (work[column : column + 1] * inverse)
        if column + AHEAD + 1 < order:
            ahead.append(wide(column + AHEAD + 1))
    eye = (rows == lax.broadcasted_iota(jnp.int32, (order, order), 1)).astype(F32)
    diagonal = jnp.sum(work[:, :order] * eye, axis=1, keepdims=True)
    coeffs = (work[:, order:] / diagonal).T
    solution_out[...] = solution_ref[...] + jnp.dot(coeffs, residual_ref[...], precision=FULL, preferred_element_type=F32)
    residual_out[...] = residual_ref[...] - jnp.dot(coeffs, image_ref[...], precision=FULL, preferred_element_type=F32)


def step_of(points, solution, residual, near_leaves, node_skeleton, upper_skeleton, far_nodes):
    row_total = lax.axis_size("gx")
    column_total = lax.axis_size("gy")
    device_total = row_total * column_total
    leaf_dev = near_leaves.shape[0]
    near = near_leaves.shape[1]
    count, depth = points.shape
    width = residual.shape[1]
    leaf = count // leaf_dev
    rank = node_skeleton.shape[1]
    points_t = points.T
    residual_t = residual.T
    solution_t = solution.T
    near_block = jnp.concatenate([points_t, residual_t.astype(BF)], axis=0)
    top = column_total // 2
    near_blocks = {}

    def send(step, block):
        return lax.ppermute(block, "gy", [(i, i ^ step) for i in range(column_total)])

    near_blocks[top] = send(top, near_block)
    near_blocks[1] = send(1, near_block)
    for step in range(top + 2, column_total, 2):
        near_blocks[step] = send(step, near_block)
    near_blocks[top + 1] = send(1, near_blocks[top])
    for step in range(2, top, 2):
        near_blocks[step] = send(step, near_block)
        near_blocks[step + 1] = send(step, near_blocks[1])
    for step in range(top + 2, column_total, 2):
        near_blocks[step + 1] = send(1, near_blocks[step])
    deep = depth + EXTRA

    blocks, right = pl.pallas_call(
        skeleton_body,
        out_shape=(
            jax.ShapeDtypeStruct((column_total, depth + width, rank), BF),
            jax.ShapeDtypeStruct((deep, count), BF),
        ),
        in_specs=vmem(3),
        out_specs=tuple(vmem(2)),
        compiler_params=pltpu.CompilerParams(vmem_limit_bytes=GRANT),
    name="skeleton",
    )(node_skeleton, points_t, residual_t)
    mine = lax.all_to_all(blocks, "gy", 0, 0)
    parts = {0: mine}
    step = row_total // 2
    while step:
        swap = [(i, i ^ step) for i in range(row_total)]
        parts.update({slot ^ step: lax.ppermute(part, "gx", swap) for slot, part in parts.items()})
        step //= 2
    parts = [parts[slot] for slot in range(row_total)]
    partial_t = pl.pallas_call(
        functools.partial(tree_body, leaf_dev, depth),
        out_shape=jax.ShapeDtypeStruct((width, count), F32),
        in_specs=[pl.BlockSpec(memory_space=pltpu.SMEM), *vmem(3 + row_total)],
        out_specs=vmem(1)[0],
        scratch_shapes=[
            pltpu.VMEM((2 * device_total - 1, deep + width, rank), BF),
        ],
        compiler_params=pltpu.CompilerParams(vmem_limit_bytes=GRANT),
    name="tree",
    )(far_nodes, upper_skeleton, right, near_block, *parts)
    image_t, small = pl.pallas_call(
        functools.partial(near_body, leaf_dev, depth),
        out_shape=(
            jax.ShapeDtypeStruct((width, count), F32),
            jax.ShapeDtypeStruct((device_total, width // 2, 4 * width), F32),
        ),
        in_specs=[
            pl.BlockSpec(memory_space=pltpu.SMEM),
            *vmem(3 + column_total - 1),
        ],
        out_specs=tuple(vmem(2)),
        scratch_shapes=[
            pltpu.VMEM((leaf_dev * near, depth + width, leaf), BF),
            pltpu.SemaphoreType.DMA((leaf_dev * near,)),
        ],
        compiler_params=pltpu.CompilerParams(vmem_limit_bytes=GRANT),
        name="near",
    )(near_leaves, right, partial_t, residual_t, *[near_blocks[step] for step in range(1, column_total)])
    small = lax.all_to_all(small, ("gx", "gy"), 0, 0)
    solution_next, residual_next = pl.pallas_call(
        solve_body,
        out_shape=(jax.ShapeDtypeStruct((width, count), F32),) * 2,
        in_specs=vmem(4),
        out_specs=tuple(vmem(2)),
        compiler_params=pltpu.CompilerParams(vmem_limit_bytes=GRANT),
        name="solve",
    )(small, solution_t, residual_t, image_t)
    return (solution_next.T, residual_next.T, image_t.T)


def solution(mesh):
    split = P(("gx", "gy"), None)
    return jax.shard_map(
        step_of,
        mesh=mesh,
        in_specs=(split, split, split, split, split, P(), split),
        out_specs=(split, split, split),
        check_vma=False,
    )
```

```python
import functools
import math

import jax
import jax.numpy as jnp
from jax import lax
from jax.experimental import pallas as pl
from jax.experimental.pallas import tpu as pltpu
from jax.sharding import PartitionSpec as P


LAMBDA_RIDGE = 1.0
FULL = lax.Precision.HIGHEST
BF = jnp.bfloat16
F32 = jnp.float32
EXTRA = 16
GROUP = 16
AHEAD = 4
GRANT = 24 * 2**20
NT = (((1,), (1,)), ((), ()))


def vmem(count):
    return [pl.BlockSpec(memory_space=pltpu.VMEM)] * count


def pieces(value):
    high = value.astype(BF).astype(F32)
    rest = value - high
    middle = rest.astype(BF).astype(F32)
    return high, middle, (rest - middle).astype(BF).astype(F32)


def square_rows(points):
    wide = points.astype(F32)
    return jnp.sum(wide * wide, axis=0, keepdims=True)


def left_block(points):
    count = points.shape[1]
    wide = points.astype(F32)
    square = jnp.sum(wide * wide, axis=0, keepdims=True)
    extra = jnp.concatenate(
        [*pieces(square), jnp.ones((3, count), F32), jnp.zeros((EXTRA - 6, count), F32)], axis=0
    )
    return jnp.concatenate([-2.0 * wide, extra], axis=0).T.astype(BF)


def right_extra(points):
    count = points.shape[1]
    return jnp.concatenate(
        [jnp.ones((3, count), F32), *pieces(square_rows(points)), jnp.zeros((EXTRA - 6, count), F32)],
        axis=0,
    ).astype(BF)


def kernel_of(left, right, depth):
    distance = jnp.dot(left, right, preferred_element_type=F32)
    return jnp.exp2(distance * (-0.5 * math.log2(math.e) / depth))


def fields(sources, right, depth):
    left = [left_block(source[:depth]) for source in sources]
    tiles = [kernel_of(block, right, depth).astype(BF) for block in left]
    sums = [
        jnp.dot(source[depth:], tile, preferred_element_type=F32)
        for source, tile in zip(sources, tiles)
    ]
    return sum(sums[1:], sums[0])


def skeleton_body(pick_ref, points_ref, residual_ref, block_ref, right_ref):
    depth, count = points_ref.shape
    rank = pick_ref.shape[1]
    points = points_ref[...]
    onehot = (lax.broadcasted_iota(jnp.int32, (count, rank), 0) == pick_ref[...]).astype(F32).astype(BF)
    chosen = jnp.dot(points, onehot, preferred_element_type=F32).astype(BF)
    right = jnp.concatenate([points, right_extra(points)], axis=0)
    tile = kernel_of(left_block(chosen), right, depth).astype(BF)
    weights = lax.dot_general(
        residual_ref[...].astype(BF), tile, NT, preferred_element_type=F32
    ) * (1.0 / math.sqrt(count))
    block = jnp.concatenate([chosen, weights.astype(BF)], axis=0)
    for copy in range(block_ref.shape[0]):
        block_ref[copy] = block
    right_ref[...] = right


def tree_nodes(depth, pick_ref, tree_ref, nodes):
    rank = tree_ref.shape[2]
    both = [jnp.concatenate([tree_ref[2 * n + 1], tree_ref[2 * n + 2]], axis=1) for n in nodes]
    picks = [pick_ref[n] for n in nodes]
    chosen = [
        jnp.dot(b[:depth], pick, preferred_element_type=F32).astype(BF) for b, pick in zip(both, picks)
    ]
    left = [left_block(points) for points in chosen]
    tiles = [kernel_of(l, b[: depth + EXTRA], depth).astype(BF) for l, b in zip(left, both)]
    ones = jnp.ones((EXTRA, 2 * rank), F32).astype(BF)
    values = [jnp.concatenate([b[depth + EXTRA :], ones], axis=0) for b in both]
    sums = [
        lax.dot_general(v, tile, NT, preferred_element_type=F32) for v, tile in zip(values, tiles)
    ]
    width = values[0].shape[0] - EXTRA
    weights = [(s[:width] / s[width : width + 1]).astype(BF) for s in sums]
    blocks = [
        jnp.concatenate([points, right_extra(points), w], axis=0)
        for points, w in zip(chosen, weights)
    ]
    for node, block in zip(nodes, blocks):
        tree_ref[node] = block


def own_body(leaf_dev, depth, upper_ref, right_ref, own_ref, part_ref, pick_ref):
    leaf = right_ref.shape[1] // leaf_dev
    nodes, rank = upper_ref.shape
    for at in range(leaf_dev):
        where = slice(at * leaf, (at + 1) * leaf)
        part_ref[:, where] = fields([own_ref[:, where]], right_ref[:, where], depth) * (
            1.0 / math.sqrt(leaf)
        )
    lanes = lax.broadcasted_iota(jnp.int32, (2 * rank, rank), 0)

    def pick(node, carry):
        pick_ref[node] = (lanes == upper_ref[pl.ds(node, 1), :]).astype(F32).astype(BF)
        return carry

    lax.fori_loop(0, nodes, pick, 0)


def tree_body(leaf_dev, depth, far_ref, pick_ref, right_ref, own_ref, *refs):
    part_refs, out_ref, tree_ref = refs[:-2], refs[-2], refs[-1]
    row_total = len(part_refs)
    column_total = part_refs[0].shape[0]
    low = row_total * column_total - 1
    mine = lax.axis_index("gx")
    for slot, part_ref in enumerate(part_refs):
        first = low + lax.bitwise_xor(mine, slot) * column_total
        blocks = [part_ref[column] for column in range(column_total)]
        extras = [right_extra(block[:depth]) for block in blocks]
        for column, (block, extra) in enumerate(zip(blocks, extras)):
            tree_ref[first + column, :depth] = block[:depth]
            tree_ref[first + column, depth : depth + EXTRA] = extra
            tree_ref[first + column, depth + EXTRA :] = block[depth:]
    while low:
        low = (low - 1) // 2
        count = low + 1
        size = min(count, GROUP)

        def level(step, carry, low=low, size=size):
            tree_nodes(depth, pick_ref, tree_ref, [low + step * size + k for k in range(size)])
            return carry

        if count == size:
            level(0, 0)
        else:
            lax.fori_loop(0, count // size, level, 0)

    leaf = right_ref.shape[1] // leaf_dev
    rank = tree_ref.shape[2]
    far = far_ref.shape[1]
    each = leaf // rank
    for at in range(leaf_dev):
        where = slice(at * leaf, (at + 1) * leaf)
        sources = []
        for first in range(0, far, each):
            both = jnp.concatenate([tree_ref[far_ref[at, first + k]] for k in range(each)], axis=1)
            sources.append(jnp.concatenate([both[:depth], both[depth + EXTRA :]], axis=0))
        out_ref[:, where] = own_ref[:, where] + fields(sources, right_ref[:, where], depth) * (1.0 / rank)


def near_body(leaf_dev, depth, near_ref, right_ref, part_ref, residual_ref, *refs):
    block_refs = refs[:-4]
    image_ref, small_ref, held, sems = refs[-4:]
    leaf = right_ref.shape[1] // leaf_dev
    near = near_ref.shape[1]
    mine = lax.axis_index("gy")
    columns = len(block_refs) + 1
    total = leaf_dev * near
    for request in range(total):
        wanted = near_ref[request // near, request % near]
        slot = lax.bitwise_xor(lax.rem(wanted // leaf_dev, columns), mine)
        inner = lax.rem(wanted, leaf_dev)
        for at, block_ref in enumerate(block_refs):

            @pl.when(slot == at + 1)
            def _(block_ref=block_ref, inner=inner, request=request):
                source = block_ref.at[:, pl.ds(pl.multiple_of(inner * leaf, leaf), leaf)]
                pltpu.make_async_copy(source, held.at[request], sems.at[request]).start()

    for at in range(leaf_dev):
        requests = range(at * near, (at + 1) * near)
        for request in requests:
            pltpu.make_async_copy(
                block_refs[0].at[:, :leaf], held.at[request], sems.at[request]
            ).wait()
        where = slice(at * leaf, (at + 1) * leaf)
        total = fields([held[request] for request in requests], right_ref[:, where], depth)
        image_ref[:, where] = (
            LAMBDA_RIDGE * residual_ref[:, where]
            + part_ref[:, where]
            + total * (1.0 / math.sqrt(leaf))
        )
    image = image_ref[...]
    gram = lax.dot_general(image, image, NT, precision=FULL, preferred_element_type=F32)
    cross = lax.dot_general(image, residual_ref[...], NT, precision=FULL, preferred_element_type=F32)
    half = gram.shape[0] // 2
    packed = jnp.concatenate([gram[:half], gram[half:], cross[:half], cross[half:]], axis=1)

    def copy(at, carry):
        small_ref[at] = packed
        return carry

    lax.fori_loop(0, small_ref.shape[0], copy, 0, unroll=8)


def solve_body(small_ref, solution_ref, residual_ref, image_ref, solution_out, residual_out):
    order = solution_ref.shape[0]
    packed = small_ref[0]
    for at in range(1, small_ref.shape[0]):
        packed = packed + small_ref[at]
    gram = jnp.concatenate([packed[:, :order], packed[:, order : 2 * order]], axis=0)
    cross = jnp.concatenate([packed[:, 2 * order : 3 * order], packed[:, 3 * order :]], axis=0)
    work = jnp.concatenate([gram, cross], axis=1)
    rows = lax.broadcasted_iota(jnp.int32, (order, 1), 0)

    def wide(column):
        return jnp.broadcast_to(work[:, column : column + 1], work.shape)

    ahead = [wide(column) for column in range(min(order, AHEAD + 1))]
    for column in range(order):
        pivots = ahead.pop(0)
        inverse = 1.0 / pivots[column : column + 1]
        factor = jnp.where(rows == column, 0.0, pivots)
        ahead = [later - factor * (later[column : column + 1] * inverse) for later in ahead]
        work = work - factor * (work[column : column + 1] * inverse)
        if column + AHEAD + 1 < order:
            ahead.append(wide(column + AHEAD + 1))
    eye = (rows == lax.broadcasted_iota(jnp.int32, (order, order), 1)).astype(F32)
    diagonal = jnp.sum(work[:, :order] * eye, axis=1, keepdims=True)
    coeffs = (work[:, order:] / diagonal).T
    solution_out[...] = solution_ref[...] + jnp.dot(coeffs, residual_ref[...], precision=FULL, preferred_element_type=F32)
    residual_out[...] = residual_ref[...] - jnp.dot(coeffs, image_ref[...], precision=FULL, preferred_element_type=F32)


def step_of(points, solution, residual, near_leaves, node_skeleton, upper_skeleton, far_nodes):
    row_total = lax.axis_size("gx")
    column_total = lax.axis_size("gy")
    device_total = row_total * column_total
    leaf_dev = near_leaves.shape[0]
    near = near_leaves.shape[1]
    count, depth = points.shape
    width = residual.shape[1]
    leaf = count // leaf_dev
    rank = node_skeleton.shape[1]
    points_t = points.T
    residual_t = residual.T
    solution_t = solution.T
    near_block = jnp.concatenate([points_t, residual_t.astype(BF)], axis=0)
    top = column_total // 2
    near_blocks = {}

    def send(step, block):
        return lax.ppermute(block, "gy", [(i, i ^ step) for i in range(column_total)])

    near_blocks[top] = send(top, near_block)
    near_blocks[1] = send(1, near_block)
    deep = depth + EXTRA

    blocks, right = pl.pallas_call(
        skeleton_body,
        out_shape=(
            jax.ShapeDtypeStruct((column_total, depth + width, rank), BF),
            jax.ShapeDtypeStruct((deep, count), BF),
        ),
        in_specs=vmem(3),
        out_specs=tuple(vmem(2)),
        compiler_params=pltpu.CompilerParams(vmem_limit_bytes=GRANT),
    name="skeleton",
    )(node_skeleton, points_t, residual_t)
    mine = lax.all_to_all(blocks, "gy", 0, 0)
    mine, late_block = lax.optimization_barrier((mine, near_block))
    for step in range(top + 2, column_total, 2):
        near_blocks[step] = send(step, late_block)
    near_blocks[top + 1] = send(1, near_blocks[top])
    for step in range(2, top, 2):
        near_blocks[step] = send(step, near_block)
        near_blocks[step + 1] = send(step, near_blocks[1])
    for step in range(top + 2, column_total, 2):
        near_blocks[step + 1] = send(1, near_blocks[step])
    parts = {0: mine}
    step = row_total // 2
    while step:
        swap = [(i, i ^ step) for i in range(row_total)]
        parts.update({slot ^ step: lax.ppermute(part, "gx", swap) for slot, part in parts.items()})
        step //= 2
    parts = [parts[slot] for slot in range(row_total)]
    own_part, picks = pl.pallas_call(
        functools.partial(own_body, leaf_dev, depth),
        out_shape=(
            jax.ShapeDtypeStruct((width, count), F32),
            jax.ShapeDtypeStruct((device_total - 1, 2 * rank, rank), BF),
        ),
        in_specs=vmem(3),
        out_specs=tuple(vmem(2)),
        compiler_params=pltpu.CompilerParams(vmem_limit_bytes=GRANT),
        name="own",
    )(upper_skeleton, right, near_block)
    partial_t = pl.pallas_call(
        functools.partial(tree_body, leaf_dev, depth),
        out_shape=jax.ShapeDtypeStruct((width, count), F32),
        in_specs=[pl.BlockSpec(memory_space=pltpu.SMEM), *vmem(3 + row_total)],
        out_specs=vmem(1)[0],
        scratch_shapes=[
            pltpu.VMEM((2 * device_total - 1, deep + width, rank), BF),
        ],
        compiler_params=pltpu.CompilerParams(vmem_limit_bytes=GRANT),
    name="tree",
    )(far_nodes, picks, right, own_part, *parts)
    image_t, small = pl.pallas_call(
        functools.partial(near_body, leaf_dev, depth),
        out_shape=(
            jax.ShapeDtypeStruct((width, count), F32),
            jax.ShapeDtypeStruct((device_total, width // 2, 4 * width), F32),
        ),
        in_specs=[
            pl.BlockSpec(memory_space=pltpu.SMEM),
            *vmem(3 + column_total - 1),
        ],
        out_specs=tuple(vmem(2)),
        scratch_shapes=[
            pltpu.VMEM((leaf_dev * near, depth + width, leaf), BF),
            pltpu.SemaphoreType.DMA((leaf_dev * near,)),
        ],
        compiler_params=pltpu.CompilerParams(vmem_limit_bytes=GRANT),
        name="near",
    )(near_leaves, right, partial_t, residual_t, *[near_blocks[step] for step in range(1, column_total)])
    small = lax.all_to_all(small, ("gx", "gy"), 0, 0)
    solution_next, residual_next = pl.pallas_call(
        solve_body,
        out_shape=(jax.ShapeDtypeStruct((width, count), F32),) * 2,
        in_specs=vmem(4),
        out_specs=tuple(vmem(2)),
        compiler_params=pltpu.CompilerParams(vmem_limit_bytes=GRANT),
        name="solve",
    )(small, solution_t, residual_t, image_t)
    return (solution_next.T, residual_next.T, image_t.T)


def solution(mesh):
    split = P(("gx", "gy"), None)
    return jax.shard_map(
        step_of,
        mesh=mesh,
        in_specs=(split, split, split, split, split, P(), split),
        out_specs=(split, split, split),
        check_vma=False,
    )
```

```python
import functools
import math

import jax
import jax.numpy as jnp
from jax import lax
from jax.experimental import pallas as pl
from jax.experimental.pallas import tpu as pltpu
from jax.sharding import PartitionSpec as P


LAMBDA_RIDGE = 1.0
FULL = lax.Precision.HIGHEST
BF = jnp.bfloat16
F32 = jnp.float32
EXTRA = 16
GROUP = 16
AHEAD = 4
GRANT = 24 * 2**20
NT = (((1,), (1,)), ((), ()))


def vmem(count):
    return [pl.BlockSpec(memory_space=pltpu.VMEM)] * count


def pieces(value):
    high = value.astype(BF).astype(F32)
    rest = value - high
    middle = rest.astype(BF).astype(F32)
    return high, middle, (rest - middle).astype(BF).astype(F32)


def square_rows(points):
    wide = points.astype(F32)
    return jnp.sum(wide * wide, axis=0, keepdims=True)


def left_block(points):
    count = points.shape[1]
    wide = points.astype(F32)
    square = jnp.sum(wide * wide, axis=0, keepdims=True)
    extra = jnp.concatenate(
        [*pieces(square), jnp.ones((3, count), F32), jnp.zeros((EXTRA - 6, count), F32)], axis=0
    )
    return jnp.concatenate([-2.0 * wide, extra], axis=0).T.astype(BF)


def right_extra(points):
    count = points.shape[1]
    return jnp.concatenate(
        [jnp.ones((3, count), F32), *pieces(square_rows(points)), jnp.zeros((EXTRA - 6, count), F32)],
        axis=0,
    ).astype(BF)


def kernel_of(left, right, depth):
    distance = jnp.dot(left, right, preferred_element_type=F32)
    return jnp.exp2(distance * (-0.5 * math.log2(math.e) / depth))


def fields(sources, right, depth):
    left = [left_block(source[:depth]) for source in sources]
    tiles = [kernel_of(block, right, depth).astype(BF) for block in left]
    sums = [
        jnp.dot(source[depth:], tile, preferred_element_type=F32)
        for source, tile in zip(sources, tiles)
    ]
    return sum(sums[1:], sums[0])


def skeleton_body(depth, pick_ref, near_ref, block_ref, right_ref):
    count = near_ref.shape[1]
    rank = pick_ref.shape[1]
    points = near_ref[:depth]
    onehot = (lax.broadcasted_iota(jnp.int32, (count, rank), 0) == pick_ref[...]).astype(F32).astype(BF)
    chosen = jnp.dot(points, onehot, preferred_element_type=F32).astype(BF)
    right = jnp.concatenate([points, right_extra(points)], axis=0)
    tile = kernel_of(left_block(chosen), right, depth).astype(BF)
    weights = lax.dot_general(
        near_ref[depth:], tile, NT, preferred_element_type=F32
    ) * (1.0 / math.sqrt(count))
    block = jnp.concatenate([chosen, weights.astype(BF)], axis=0)
    for copy in range(block_ref.shape[0]):
        block_ref[copy] = block
    right_ref[...] = right


def tree_nodes(depth, upper_ref, tree_ref, nodes):
    rank = tree_ref.shape[2]
    lanes = lax.broadcasted_iota(jnp.int32, (2 * rank, rank), 0)
    both = [jnp.concatenate([tree_ref[2 * n + 1], tree_ref[2 * n + 2]], axis=1) for n in nodes]
    picks = [(lanes == upper_ref[pl.ds(n, 1), :]).astype(F32).astype(BF) for n in nodes]
    chosen = [
        jnp.dot(b[:depth], pick, preferred_element_type=F32).astype(BF) for b, pick in zip(both, picks)
    ]
    left = [left_block(points) for points in chosen]
    tiles = [kernel_of(l, b[: depth + EXTRA], depth).astype(BF) for l, b in zip(left, both)]
    ones = jnp.ones((EXTRA, 2 * rank), F32).astype(BF)
    values = [jnp.concatenate([b[depth + EXTRA :], ones], axis=0) for b in both]
    sums = [
        lax.dot_general(v, tile, NT, preferred_element_type=F32) for v, tile in zip(values, tiles)
    ]
    width = values[0].shape[0] - EXTRA
    weights = [(s[:width] / s[width : width + 1]).astype(BF) for s in sums]
    blocks = [
        jnp.concatenate([points, right_extra(points), w], axis=0)
        for points, w in zip(chosen, weights)
    ]
    for node, block in zip(nodes, blocks):
        tree_ref[node] = block


def own_body(leaf_dev, depth, right_ref, own_ref, part_ref):
    leaf = right_ref.shape[1] // leaf_dev
    for at in range(leaf_dev):
        where = slice(at * leaf, (at + 1) * leaf)
        part_ref[:, where] = fields([own_ref[:, where]], right_ref[:, where], depth) * (
            1.0 / math.sqrt(leaf)
        )


def tree_body(leaf_dev, depth, far_ref, upper_ref, right_ref, own_ref, *refs):
    part_refs, out_ref, tree_ref = refs[:-2], refs[-2], refs[-1]
    row_total = len(part_refs)
    column_total = part_refs[0].shape[0]
    low = row_total * column_total - 1
    mine = lax.axis_index("gx")
    for slot, part_ref in enumerate(part_refs):
        first = low + lax.bitwise_xor(mine, slot) * column_total
        blocks = [part_ref[column] for column in range(column_total)]
        extras = [right_extra(block[:depth]) for block in blocks]
        for column, (block, extra) in enumerate(zip(blocks, extras)):
            tree_ref[first + column, :depth] = block[:depth]
            tree_ref[first + column, depth : depth + EXTRA] = extra
            tree_ref[first + column, depth + EXTRA :] = block[depth:]
    while low:
        low = (low - 1) // 2
        count = low + 1
        size = min(count, GROUP)

        def level(step, carry, low=low, size=size):
            tree_nodes(depth, upper_ref, tree_ref, [low + step * size + k for k in range(size)])
            return carry

        if count == size:
            level(0, 0)
        else:
            lax.fori_loop(0, count // size, level, 0)

    leaf = right_ref.shape[1] // leaf_dev
    rank = tree_ref.shape[2]
    far = far_ref.shape[1]
    each = leaf // rank
    for at in range(leaf_dev):
        where = slice(at * leaf, (at + 1) * leaf)
        sources = []
        for first in range(0, far, each):
            both = jnp.concatenate([tree_ref[far_ref[at, first + k]] for k in range(each)], axis=1)
            sources.append(jnp.concatenate([both[:depth], both[depth + EXTRA :]], axis=0))
        out_ref[:, where] = own_ref[:, where] + fields(sources, right_ref[:, where], depth) * (1.0 / rank)


def near_body(leaf_dev, depth, near_ref, right_ref, part_ref, residual_ref, *refs):
    block_refs = refs[:-5]
    image_ref, kept_ref, small_ref, held, sems = refs[-5:]
    leaf = right_ref.shape[1] // leaf_dev
    near = near_ref.shape[1]
    mine = lax.axis_index("gy")
    columns = len(block_refs) + 1
    total = leaf_dev * near
    for request in range(total):
        wanted = near_ref[request // near, request % near]
        slot = lax.bitwise_xor(lax.rem(wanted // leaf_dev, columns), mine)
        inner = lax.rem(wanted, leaf_dev)
        for at, block_ref in enumerate(block_refs):

            @pl.when(slot == at + 1)
            def _(block_ref=block_ref, inner=inner, request=request):
                source = block_ref.at[:, pl.ds(pl.multiple_of(inner * leaf, leaf), leaf)]
                pltpu.make_async_copy(source, held.at[request], sems.at[request]).start()

    for at in range(leaf_dev):
        requests = range(at * near, (at + 1) * near)
        for request in requests:
            pltpu.make_async_copy(
                block_refs[0].at[:, :leaf], held.at[request], sems.at[request]
            ).wait()
        where = slice(at * leaf, (at + 1) * leaf)
        total = fields([held[request] for request in requests], right_ref[:, where], depth)
        image_ref[:, where] = (
            LAMBDA_RIDGE * residual_ref[:, where]
            + part_ref[:, where]
            + total * (1.0 / math.sqrt(leaf))
        )
    image = image_ref[...]
    kept_ref[...] = image
    gram = lax.dot_general(image, image, NT, precision=FULL, preferred_element_type=F32)
    cross = lax.dot_general(image, residual_ref[...], NT, precision=FULL, preferred_element_type=F32)
    half = gram.shape[0] // 2
    packed = jnp.concatenate([gram[:half], gram[half:], cross[:half], cross[half:]], axis=1)

    def copy(at, carry):
        small_ref[at] = packed
        return carry

    lax.fori_loop(0, small_ref.shape[0], copy, 0, unroll=8)


def solve_body(small_ref, solution_ref, residual_ref, image_ref, solution_out, residual_out):
    order = solution_ref.shape[0]
    packed = small_ref[0]
    for at in range(1, small_ref.shape[0]):
        packed = packed + small_ref[at]
    gram = jnp.concatenate([packed[:, :order], packed[:, order : 2 * order]], axis=0)
    cross = jnp.concatenate([packed[:, 2 * order : 3 * order], packed[:, 3 * order :]], axis=0)
    work = jnp.concatenate([gram, cross], axis=1)
    rows = lax.broadcasted_iota(jnp.int32, (order, 1), 0)

    def wide(column):
        return jnp.broadcast_to(work[:, column : column + 1], work.shape)

    ahead = [wide(column) for column in range(min(order, AHEAD + 1))]
    for column in range(order):
        pivots = ahead.pop(0)
        inverse = 1.0 / pivots[column : column + 1]
        factor = jnp.where(rows == column, 0.0, pivots)
        ahead = [later - factor * (later[column : column + 1] * inverse) for later in ahead]
        work = work - factor * (work[column : column + 1] * inverse)
        if column + AHEAD + 1 < order:
            ahead.append(wide(column + AHEAD + 1))
    eye = (rows == lax.broadcasted_iota(jnp.int32, (order, order), 1)).astype(F32)
    diagonal = jnp.sum(work[:, :order] * eye, axis=1, keepdims=True)
    coeffs = (work[:, order:] / diagonal).T
    solution_out[...] = solution_ref[...] + jnp.dot(coeffs, residual_ref[...], precision=FULL, preferred_element_type=F32)
    residual_out[...] = residual_ref[...] - jnp.dot(coeffs, image_ref[...], precision=FULL, preferred_element_type=F32)


def step_of(points, solution, residual, near_leaves, node_skeleton, upper_skeleton, far_nodes):
    row_total = lax.axis_size("gx")
    column_total = lax.axis_size("gy")
    device_total = row_total * column_total
    leaf_dev = near_leaves.shape[0]
    near = near_leaves.shape[1]
    count, depth = points.shape
    width = residual.shape[1]
    leaf = count // leaf_dev
    rank = node_skeleton.shape[1]
    points_t = points.T
    residual_t = residual.T
    solution_t = solution.T
    near_block = jnp.concatenate([points_t, residual_t.astype(BF)], axis=0)
    top = column_total // 2
    near_blocks = {}

    def send(step, block):
        return lax.ppermute(block, "gy", [(i, i ^ step) for i in range(column_total)])

    near_blocks[top] = send(top, near_block)
    near_blocks[1] = send(1, near_block)
    near_blocks[2] = send(2, near_block)
    deep = depth + EXTRA

    blocks, right = pl.pallas_call(
        functools.partial(skeleton_body, depth),
        out_shape=(
            jax.ShapeDtypeStruct((column_total, depth + width, rank), BF),
            jax.ShapeDtypeStruct((deep, count), BF),
        ),
        in_specs=vmem(2),
        out_specs=tuple(vmem(2)),
        compiler_params=pltpu.CompilerParams(vmem_limit_bytes=GRANT),
    name="skeleton",
    )(node_skeleton, near_block)
    mine = lax.all_to_all(blocks, "gy", 0, 0)
    mine, late_block = lax.optimization_barrier((mine, near_block))
    for step in range(top + 2, column_total, 2):
        near_blocks[step] = send(step, late_block)
    near_blocks[top + 1] = send(1, near_blocks[top])
    for step in range(2, top, 2):
        if step > 2:
            near_blocks[step] = send(step, near_block)
        near_blocks[step + 1] = send(step, near_blocks[1])
    for step in range(top + 2, column_total, 2):
        near_blocks[step + 1] = send(1, near_blocks[step])
    parts = {0: mine}
    step = row_total // 2
    while step:
        swap = [(i, i ^ step) for i in range(row_total)]
        parts.update({slot ^ step: lax.ppermute(part, "gx", swap) for slot, part in parts.items()})
        step //= 2
    parts = [parts[slot] for slot in range(row_total)]
    own_part = pl.pallas_call(
        functools.partial(own_body, leaf_dev, depth),
        out_shape=jax.ShapeDtypeStruct((width, count), F32),
        in_specs=vmem(2),
        out_specs=vmem(1)[0],
        compiler_params=pltpu.CompilerParams(vmem_limit_bytes=GRANT),
        name="own",
    )(right, near_block)
    partial_t = pl.pallas_call(
        functools.partial(tree_body, leaf_dev, depth),
        out_shape=jax.ShapeDtypeStruct((width, count), F32),
        in_specs=[pl.BlockSpec(memory_space=pltpu.SMEM), *vmem(3 + row_total)],
        out_specs=vmem(1)[0],
        scratch_shapes=[
            pltpu.VMEM((2 * device_total - 1, deep + width, rank), BF),
        ],
        compiler_params=pltpu.CompilerParams(vmem_limit_bytes=GRANT),
    name="tree",
    )(far_nodes, upper_skeleton, right, own_part, *parts)
    image_t, kept_t, small = pl.pallas_call(
        functools.partial(near_body, leaf_dev, depth),
        out_shape=(
            jax.ShapeDtypeStruct((width, count), F32),
            jax.ShapeDtypeStruct((width, count), F32),
            jax.ShapeDtypeStruct((device_total, width // 2, 4 * width), F32),
        ),
        in_specs=[
            pl.BlockSpec(memory_space=pltpu.SMEM),
            *vmem(3 + column_total - 1),
        ],
        out_specs=tuple(vmem(3)),
        scratch_shapes=[
            pltpu.VMEM((leaf_dev * near, depth + width, leaf), BF),
            pltpu.SemaphoreType.DMA((leaf_dev * near,)),
        ],
        compiler_params=pltpu.CompilerParams(vmem_limit_bytes=GRANT),
        name="near",
    )(near_leaves, right, partial_t, residual_t, *[near_blocks[step] for step in range(1, column_total)])
    small = lax.all_to_all(small, ("gx", "gy"), 0, 0)
    solution_next, residual_next = pl.pallas_call(
        solve_body,
        out_shape=(jax.ShapeDtypeStruct((width, count), F32),) * 2,
        in_specs=vmem(4),
        out_specs=tuple(vmem(2)),
        compiler_params=pltpu.CompilerParams(vmem_limit_bytes=GRANT),
        name="solve",
    )(small, solution_t, residual_t, kept_t)
    return (solution_next.T, residual_next.T, image_t.T)


def solution(mesh):
    split = P(("gx", "gy"), None)
    return jax.shard_map(
        step_of,
        mesh=mesh,
        in_specs=(split, split, split, split, split, P(), split),
        out_specs=(split, split, split),
        check_vma=False,
    )
```

```python
import functools
import math

import jax
import jax.numpy as jnp
from jax import lax
from jax.experimental import pallas as pl
from jax.experimental.pallas import tpu as pltpu
from jax.sharding import PartitionSpec as P


LAMBDA_RIDGE = 1.0
FULL = lax.Precision.HIGHEST
BF = jnp.bfloat16
F32 = jnp.float32
EXTRA = 16
GROUP = 16
AHEAD = 4
GRANT = 24 * 2**20
NT = (((1,), (1,)), ((), ()))


def vmem(count):
    return [pl.BlockSpec(memory_space=pltpu.VMEM)] * count


def pieces(value):
    high = value.astype(BF).astype(F32)
    rest = value - high
    middle = rest.astype(BF).astype(F32)
    return high, middle, (rest - middle).astype(BF).astype(F32)


def square_rows(points):
    wide = points.astype(F32)
    return jnp.sum(wide * wide, axis=0, keepdims=True)


def left_block(points):
    count = points.shape[1]
    wide = points.astype(F32)
    square = jnp.sum(wide * wide, axis=0, keepdims=True)
    extra = jnp.concatenate(
        [*pieces(square), jnp.ones((3, count), F32), jnp.zeros((EXTRA - 6, count), F32)], axis=0
    )
    return jnp.concatenate([-2.0 * wide, extra], axis=0).T.astype(BF)


def right_extra(points):
    count = points.shape[1]
    return jnp.concatenate(
        [jnp.ones((3, count), F32), *pieces(square_rows(points)), jnp.zeros((EXTRA - 6, count), F32)],
        axis=0,
    ).astype(BF)


def kernel_of(left, right, depth):
    distance = jnp.dot(left, right, preferred_element_type=F32)
    return jnp.exp2(distance * (-0.5 * math.log2(math.e) / depth))


def fields(sources, right, depth):
    left = [left_block(source[:depth]) for source in sources]
    tiles = [kernel_of(block, right, depth).astype(BF) for block in left]
    sums = [
        jnp.dot(source[depth:], tile, preferred_element_type=F32)
        for source, tile in zip(sources, tiles)
    ]
    return sum(sums[1:], sums[0])


def skeleton_body(depth, pick_ref, near_ref, block_ref, right_ref):
    count = near_ref.shape[1]
    rank = pick_ref.shape[1]
    points = near_ref[:depth]
    onehot = (lax.broadcasted_iota(jnp.int32, (count, rank), 0) == pick_ref[...]).astype(F32).astype(BF)
    chosen = jnp.dot(points, onehot, preferred_element_type=F32).astype(BF)
    right = jnp.concatenate([points, right_extra(points)], axis=0)
    tile = kernel_of(left_block(chosen), right, depth).astype(BF)
    weights = lax.dot_general(
        near_ref[depth:], tile, NT, preferred_element_type=F32
    ) * (1.0 / math.sqrt(count))
    block = jnp.concatenate([chosen, weights.astype(BF)], axis=0)
    for copy in range(block_ref.shape[0]):
        block_ref[copy] = block
    right_ref[...] = right


def tree_nodes(depth, upper_ref, tree_ref, nodes):
    rank = tree_ref.shape[2]
    lanes = lax.broadcasted_iota(jnp.int32, (2 * rank, rank), 0)
    both = [jnp.concatenate([tree_ref[2 * n + 1], tree_ref[2 * n + 2]], axis=1) for n in nodes]
    picks = [(lanes == upper_ref[pl.ds(n, 1), :]).astype(F32).astype(BF) for n in nodes]
    chosen = [
        jnp.dot(b[:depth], pick, preferred_element_type=F32).astype(BF) for b, pick in zip(both, picks)
    ]
    left = [left_block(points) for points in chosen]
    tiles = [kernel_of(l, b[: depth + EXTRA], depth).astype(BF) for l, b in zip(left, both)]
    ones = jnp.ones((EXTRA, 2 * rank), F32).astype(BF)
    values = [jnp.concatenate([b[depth + EXTRA :], ones], axis=0) for b in both]
    sums = [
        lax.dot_general(v, tile, NT, preferred_element_type=F32) for v, tile in zip(values, tiles)
    ]
    width = values[0].shape[0] - EXTRA
    weights = [(s[:width] / s[width : width + 1]).astype(BF) for s in sums]
    blocks = [
        jnp.concatenate([points, right_extra(points), w], axis=0)
        for points, w in zip(chosen, weights)
    ]
    for node, block in zip(nodes, blocks):
        tree_ref[node] = block


def own_body(leaf_dev, depth, right_ref, own_ref, part_ref):
    leaf = right_ref.shape[1] // leaf_dev
    for at in range(leaf_dev):
        where = slice(at * leaf, (at + 1) * leaf)
        part_ref[:, where] = fields([own_ref[:, where]], right_ref[:, where], depth) * (
            1.0 / math.sqrt(leaf)
        )


def tree_body(leaf_dev, depth, far_ref, near_ref, upper_ref, right_ref, own_ref, *refs):
    part_refs, out_ref, tree_ref = refs[:-2], refs[-2], refs[-1]
    row_total = len(part_refs)
    column_total = part_refs[0].shape[0]
    low = row_total * column_total - 1
    mine = lax.axis_index("gx")
    for slot, part_ref in enumerate(part_refs):
        first = low + lax.bitwise_xor(mine, slot) * column_total
        blocks = [part_ref[column] for column in range(column_total)]
        extras = [right_extra(block[:depth]) for block in blocks]
        for column, (block, extra) in enumerate(zip(blocks, extras)):
            tree_ref[first + column, :depth] = block[:depth]
            tree_ref[first + column, depth : depth + EXTRA] = extra
            tree_ref[first + column, depth + EXTRA :] = block[depth:]
    while low:
        low = (low - 1) // 2
        count = low + 1
        size = min(count, GROUP)

        def level(step, carry, low=low, size=size):
            tree_nodes(depth, upper_ref, tree_ref, [low + step * size + k for k in range(size)])
            return carry

        if count == size:
            level(0, 0)
        else:
            lax.fori_loop(0, count // size, level, 0)

    leaf = right_ref.shape[1] // leaf_dev
    rank = tree_ref.shape[2]
    far = far_ref.shape[1]
    each = leaf // rank
    for at in range(leaf_dev):
        where = slice(at * leaf, (at + 1) * leaf)
        sources = []
        for first in range(0, far, each):
            both = jnp.concatenate([tree_ref[far_ref[at, first + k]] for k in range(each)], axis=1)
            sources.append(jnp.concatenate([both[:depth], both[depth + EXTRA :]], axis=0))
        out_ref[:, where] = own_ref[:, where] + fields(sources, right_ref[:, where], depth) * (1.0 / rank)


def near_body(leaf_dev, depth, near_ref, right_ref, part_ref, residual_ref, *refs):
    block_refs = refs[:-5]
    image_ref, kept_ref, small_ref, held, sems = refs[-5:]
    leaf = right_ref.shape[1] // leaf_dev
    near = near_ref.shape[1]
    mine = lax.axis_index("gy")
    columns = len(block_refs) + 1
    total = leaf_dev * near
    for request in range(total):
        wanted = near_ref[request // near, request % near]
        slot = lax.bitwise_xor(lax.rem(wanted // leaf_dev, columns), mine)
        inner = lax.rem(wanted, leaf_dev)
        for at, block_ref in enumerate(block_refs):

            @pl.when(slot == at + 1)
            def _(block_ref=block_ref, inner=inner, request=request):
                source = block_ref.at[:, pl.ds(pl.multiple_of(inner * leaf, leaf), leaf)]
                pltpu.make_async_copy(source, held.at[request], sems.at[request]).start()

    for at in range(leaf_dev):
        requests = range(at * near, (at + 1) * near)
        for request in requests:
            pltpu.make_async_copy(
                block_refs[0].at[:, :leaf], held.at[request], sems.at[request]
            ).wait()
        where = slice(at * leaf, (at + 1) * leaf)
        total = fields([held[request] for request in requests], right_ref[:, where], depth)
        image_ref[:, where] = (
            LAMBDA_RIDGE * residual_ref[:, where]
            + part_ref[:, where]
            + total * (1.0 / math.sqrt(leaf))
        )
    image = image_ref[...]
    kept_ref[...] = image
    gram = lax.dot_general(image, image, NT, precision=FULL, preferred_element_type=F32)
    cross = lax.dot_general(image, residual_ref[...], NT, precision=FULL, preferred_element_type=F32)
    half = gram.shape[0] // 2
    packed = jnp.concatenate([gram[:half], gram[half:], cross[:half], cross[half:]], axis=1)

    def copy(at, carry):
        small_ref[at] = packed
        return carry

    lax.fori_loop(0, small_ref.shape[0], copy, 0, unroll=8)


def solve_body(small_ref, solution_ref, residual_ref, image_ref, solution_out, residual_out):
    order = solution_ref.shape[0]
    packed = small_ref[0]
    for at in range(1, small_ref.shape[0]):
        packed = packed + small_ref[at]
    gram = jnp.concatenate([packed[:, :order], packed[:, order : 2 * order]], axis=0)
    cross = jnp.concatenate([packed[:, 2 * order : 3 * order], packed[:, 3 * order :]], axis=0)
    work = jnp.concatenate([gram, cross], axis=1)
    rows = lax.broadcasted_iota(jnp.int32, (order, 1), 0)

    def wide(column):
        return jnp.broadcast_to(work[:, column : column + 1], work.shape)

    ahead = [wide(column) for column in range(min(order, AHEAD + 1))]
    for column in range(order):
        pivots = ahead.pop(0)
        inverse = 1.0 / pivots[column : column + 1]
        factor = jnp.where(rows == column, 0.0, pivots)
        ahead = [later - factor * (later[column : column + 1] * inverse) for later in ahead]
        work = work - factor * (work[column : column + 1] * inverse)
        if column + AHEAD + 1 < order:
            ahead.append(wide(column + AHEAD + 1))
    eye = (rows == lax.broadcasted_iota(jnp.int32, (order, order), 1)).astype(F32)
    diagonal = jnp.sum(work[:, :order] * eye, axis=1, keepdims=True)
    coeffs = (work[:, order:] / diagonal).T
    solution_out[...] = solution_ref[...] + jnp.dot(coeffs, residual_ref[...], precision=FULL, preferred_element_type=F32)
    residual_out[...] = residual_ref[...] - jnp.dot(coeffs, image_ref[...], precision=FULL, preferred_element_type=F32)


def step_of(points, solution, residual, near_leaves, node_skeleton, upper_skeleton, far_nodes):
    row_total = lax.axis_size("gx")
    column_total = lax.axis_size("gy")
    device_total = row_total * column_total
    leaf_dev = near_leaves.shape[0]
    near = near_leaves.shape[1]
    count, depth = points.shape
    width = residual.shape[1]
    leaf = count // leaf_dev
    rank = node_skeleton.shape[1]
    points_t = points.T
    residual_t = residual.T
    solution_t = solution.T
    near_block = jnp.concatenate([points_t, residual_t.astype(BF)], axis=0)
    top = column_total // 2
    near_blocks = {}

    def send(step, block):
        return lax.ppermute(block, "gy", [(i, i ^ step) for i in range(column_total)])

    near_blocks[top] = send(top, near_block)
    near_blocks[1] = send(1, near_block)
    near_blocks[2] = send(2, near_block)
    deep = depth + EXTRA

    blocks, right = pl.pallas_call(
        functools.partial(skeleton_body, depth),
        out_shape=(
            jax.ShapeDtypeStruct((column_total, depth + width, rank), BF),
            jax.ShapeDtypeStruct((deep, count), BF),
        ),
        in_specs=vmem(2),
        out_specs=tuple(vmem(2)),
        compiler_params=pltpu.CompilerParams(vmem_limit_bytes=GRANT),
    name="skeleton",
    )(node_skeleton, near_block)
    mine = lax.all_to_all(blocks, "gy", 0, 0)
    mine, late_block = lax.optimization_barrier((mine, near_block))
    for step in range(top + 2, column_total, 2):
        near_blocks[step] = send(step, late_block)
    near_blocks[top + 1] = send(1, near_blocks[top])
    for step in range(2, top, 2):
        if step > 2:
            near_blocks[step] = send(step, near_block)
        near_blocks[step + 1] = send(step, near_blocks[1])
    for step in range(top + 2, column_total, 2):
        near_blocks[step + 1] = send(1, near_blocks[step])
    parts = {0: mine}
    step = row_total // 2
    while step:
        swap = [(i, i ^ step) for i in range(row_total)]
        parts.update({slot ^ step: lax.ppermute(part, "gx", swap) for slot, part in parts.items()})
        step //= 2
    parts = [parts[slot] for slot in range(row_total)]
    own_part = pl.pallas_call(
        functools.partial(own_body, leaf_dev, depth),
        out_shape=jax.ShapeDtypeStruct((width, count), F32),
        in_specs=vmem(2),
        out_specs=vmem(1)[0],
        compiler_params=pltpu.CompilerParams(vmem_limit_bytes=GRANT),
        name="own",
    )(right, near_block)
    partial_t = pl.pallas_call(
        functools.partial(tree_body, leaf_dev, depth),
        out_shape=jax.ShapeDtypeStruct((width, count), F32),
        in_specs=[*[pl.BlockSpec(memory_space=pltpu.SMEM)] * 2, *vmem(3 + row_total)],
        out_specs=vmem(1)[0],
        scratch_shapes=[
            pltpu.VMEM((2 * device_total - 1, deep + width, rank), BF),
        ],
        compiler_params=pltpu.CompilerParams(vmem_limit_bytes=GRANT),
    name="tree",
    )(far_nodes, near_leaves, upper_skeleton, right, own_part, *parts)
    image_t, kept_t, small = pl.pallas_call(
        functools.partial(near_body, leaf_dev, depth),
        out_shape=(
            jax.ShapeDtypeStruct((width, count), F32),
            jax.ShapeDtypeStruct((width, count), F32),
            jax.ShapeDtypeStruct((device_total, width // 2, 4 * width), F32),
        ),
        in_specs=[
            pl.BlockSpec(memory_space=pltpu.SMEM),
            *vmem(3 + column_total - 1),
        ],
        out_specs=tuple(vmem(3)),
        scratch_shapes=[
            pltpu.VMEM((leaf_dev * near, depth + width, leaf), BF),
            pltpu.SemaphoreType.DMA((leaf_dev * near,)),
        ],
        compiler_params=pltpu.CompilerParams(vmem_limit_bytes=GRANT),
        name="near",
    )(near_leaves, right, partial_t, residual_t, *[near_blocks[step] for step in range(1, column_total)])
    small = lax.all_to_all(small, ("gx", "gy"), 0, 0)
    solution_next, residual_next = pl.pallas_call(
        solve_body,
        out_shape=(jax.ShapeDtypeStruct((width, count), F32),) * 2,
        in_specs=vmem(4),
        out_specs=tuple(vmem(2)),
        compiler_params=pltpu.CompilerParams(vmem_limit_bytes=GRANT),
        name="solve",
    )(small, solution_t, residual_t, kept_t)
    return (solution_next.T, residual_next.T, image_t.T)


def solution(mesh):
    split = P(("gx", "gy"), None)
    return jax.shard_map(
        step_of,
        mesh=mesh,
        in_specs=(split, split, split, split, split, P(), split),
        out_specs=(split, split, split),
        check_vma=False,
    )
```
